256 devices in a mesh: tok: 4 (over y), smp: 64 (over x, z, core).
Axes of the slice: x: 4, y: 4, z: 8, core: 2. Of those that a mesh axis runs over, the one named last changes fastest.
Arguments:
- row_table: float32 [8, 16384, 384], P('tok', 'smp'), may hold values from -6 to 6
- row_accum: float32 [8, 16384], P('tok', 'smp'), may hold values from 0.0001 to 0.01
- last_step: int32 [8, 16384], P('tok', 'smp'), may hold values from 0 to 47
- step_now: int32 [1], replicated, may hold values from 48 to 63
- row_ids: int32 [8, 64, 64, 2], P('tok', 'smp'), may hold values from 0 to 255, as said below
- row_counts: int32 [8, 64, 64], P('tok', 'smp'), may hold values from 1 to 2, as said below
- sample_slots: int32 [8, 16384], P(None, 'smp'), may hold values from 0 to 127, as said below
- labels: int32 [16384], P('smp'), may hold values 0 or 1
- up_weight: bfloat16 [384, 8, 1536], P('smp', 'tok'), may hold values from -0.3125 to 0.3125
- down_weight: bfloat16 [384, 8, 1536], P('smp', 'tok'), may hold values from -0.15625 to 0.15625
- out_weight: float32 [8, 384], P('tok'), may hold values from -0.3125 to 0.3125
Outputs:
- new_table: float32 [8, 16384, 384], P('tok', 'smp')
- new_accum: float32 [8, 16384], P('tok', 'smp')
- grad_down: float32 [384, 8, 1536], P('smp', 'tok')
- logits: float32 [16384], P('smp')
The draws below stay inside these ranges and needn't reach their ends.
Inputs may be any that keep to these rules, and one draw needn't show every extreme that they name: The first row_counts[t, o, g] entries of each list are distinct; later entries are padding; every token and owner has a list of 2 valid entries for some group. `row_ids`: row numbers within the owner's shard. `sample_slots`: each slot o * 2 + c names a valid entry c < row_counts[t, o, s // 256]. `last_step`: each row's last step is before step_now.
All inputs are finite; a program needn't handle non-finite values. No bound on the sum of `labels` on one device may be relied on, other than what follows from the above.
Results may differ from the reference program's by a relative error of at most 0.0021.
Values may be sent and summed in bfloat16 or wider, within the bound.
No kernel may reach another device: no remote copies, remote signals or barrier semaphores. Data moves between devices by JAX's collectives and lax.ppermute only.
A program may use at most 64 MiB of HBM per device.

```python
import math
import jax
import jax.numpy as jnp
from jax import lax

D = 384
FF = 1536
TOKS = 8
BATCH = 256
CAP = 2
ROWS_DEV = 256
HEAD = 48
SAMPLES = 16384
ROWS = 16384
N_SMP = 64


def list_counts(key):
    base_key = jax.random.fold_in(key, 701)
    first_key = jax.random.fold_in(base_key, 1)
    second_key = jax.random.fold_in(base_key, 2)
    counts = jax.random.randint(first_key, (TOKS, N_SMP, N_SMP), 1, CAP + 1, dtype=jnp.int32)
    chosen = jax.random.randint(second_key, (TOKS, N_SMP), 0, N_SMP, dtype=jnp.int32)
    group_range = jnp.arange(N_SMP, dtype=jnp.int32)
    return jnp.where(group_range[None, None, :] == chosen[:, :, None], CAP, counts).astype(jnp.int32)


def draw_row_counts(key, part):
    return list_counts(key)


def draw_row_ids(key, part):
    base_key = jax.random.fold_in(key, 702)
    first_key = jax.random.fold_in(base_key, 1)
    second_key = jax.random.fold_in(base_key, 2)
    starts = jax.random.randint(first_key, (TOKS, N_SMP, N_SMP, 1), 0, ROWS_DEV, dtype=jnp.int32)
    strides = jax.random.randint(second_key, (TOKS, N_SMP, N_SMP, 1), 1, ROWS_DEV // CAP + 1, dtype=jnp.int32)
    offsets = jnp.arange(CAP, dtype=jnp.int32)[None, None, None, :]
    return ((starts + strides * offsets) % ROWS_DEV).astype(jnp.int32)


def draw_sample_slots(key, part):
    counts = list_counts(key)
    base_key = jax.random.fold_in(key, 703)
    first_key = jax.random.fold_in(base_key, 1)
    second_key = jax.random.fold_in(base_key, 2)
    owners = jax.random.randint(first_key, (TOKS, SAMPLES), 0, N_SMP, dtype=jnp.int32)
    groups = (jnp.arange(SAMPLES, dtype=jnp.int32) // BATCH)[None, :]
    tok_range = jnp.arange(TOKS, dtype=jnp.int32)[:, None]
    limits = counts[tok_range, owners, groups]
    within = jax.random.randint(second_key, (TOKS, SAMPLES), 0, limits, dtype=jnp.int32)
    return (owners * CAP + within).astype(jnp.int32)


def set_ends(result, own_key, least, largest):
    longest = result.shape.index(max(result.shape))
    spots = []
    for shift in (0, 1):
        where = [jax.random.randint(jax.random.fold_in(own_key, axis), (), 0, length) for axis, length in enumerate(result.shape)]
        where[longest] = (where[longest] + shift) % result.shape[longest]
        spots.append(tuple(where))
    return result.at[spots[0]].set(least).at[spots[1]].set(largest)


def levels(rng, shape, pieces, low, top_value):
    def one(position, shards_of):
        draws = jax.random.uniform(jax.random.fold_in(jax.random.fold_in(rng, 6), position), (shards_of,), jnp.float32, low / len(pieces), top_value / len(pieces))
        return jnp.repeat(jnp.exp(draws), shape[position] // shards_of).reshape((-1,) + (1,) * (len(shape) - position - 1))

    loudness = one(*pieces[0])
    for cut in pieces[1:]:
        loudness = loudness * one(*cut)
    return loudness


def normal_values(stream_key, shape, spread, limit, cuts=(), kind=jnp.bfloat16):
    array = jax.random.normal(stream_key, shape, jnp.float32) * spread
    if len(cuts) > 0:
        array = levels(stream_key, shape, cuts, -0.22, 0.18) * array
    return jnp.clip(array, min=-limit, max=limit).astype(kind)


def setup_inputs(seed: int = 0) -> dict:
    streams_of = jax.random.split(jax.random.key(seed), 12)
    return {
        "row_table": normal_values(streams_of[0], (TOKS, ROWS, D), 1.0, 6.0, ((0, 4), (1, 64)), jnp.float32),
        "row_accum": jnp.clip(jnp.exp(math.log(0.01) - 4.6051702 * jax.random.uniform(streams_of[1], (TOKS, ROWS), jnp.float32) ** levels(streams_of[1], (TOKS, ROWS), ((0, 4), (1, 64)), -0.2, 0.2)), 0.0001, 0.01),
        "last_step": set_ends(jax.random.randint(streams_of[2], (TOKS, ROWS), 0, 48), jax.random.fold_in(streams_of[2], 1), 0, 47).astype(jnp.int32),
        "step_now": jax.random.randint(streams_of[3], (1,), 48, 64).astype(jnp.int32),
        "row_ids": draw_row_ids(jax.random.fold_in(streams_of[11], 71), 0),
        "row_counts": draw_row_counts(jax.random.fold_in(streams_of[11], 71), 0),
        "sample_slots": draw_sample_slots(jax.random.fold_in(streams_of[11], 71), 0),
        "labels": set_ends((jax.random.randint(streams_of[7], (SAMPLES,), 0, 2) < 1).astype(jnp.int32), jax.random.fold_in(streams_of[7], 1), 0, 1),
        "up_weight": normal_values(streams_of[8], (D, TOKS, FF), D ** -0.5, 0.3125, ((0, 64), (1, 4))),
        "down_weight": normal_values(streams_of[9], (D, TOKS, FF), FF ** -0.5, 0.15625, ((0, 64), (1, 4))),
        "out_weight": normal_values(streams_of[10], (TOKS, D), D ** -0.5, 0.3125, ((0, 4),), jnp.float32),
    }


decay_log = math.log(0.98)
learn_rate = 0.2
norm_eps = 1e-05

def normalize(values):
    centre = lax.optimization_barrier(jnp.mean(values, axis=-1, keepdims=True))
    shifted = values - centre
    inverse = lax.rsqrt(lax.optimization_barrier(jnp.mean(shifted * shifted, axis=-1, keepdims=True)) + norm_eps)
    return (shifted * inverse, inverse)

def norm_back(grad_in, normed, inverse):
    first_mean = lax.optimization_barrier(jnp.mean(grad_in, axis=-1, keepdims=True))
    second = lax.optimization_barrier(jnp.mean(grad_in * normed, axis=-1, keepdims=True))
    return inverse * (grad_in - first_mean - normed * second)

def gelu_grad(preact):
    cumulative = 0.5 * (1.0 + lax.erf(preact * (1.0 / math.sqrt(2.0))))
    density = jnp.exp(-0.5 * preact * preact) * (1.0 / math.sqrt(2.0 * math.pi))
    return cumulative + preact * density

def swap_heads(values):
    return values.reshape(TOKS, SAMPLES, TOKS, HEAD).transpose(2, 1, 0, 3).reshape(TOKS, SAMPLES, D)

def reference(row_table, row_accum, last_step, step_now, row_ids, row_counts, sample_slots, labels, up_weight, down_weight, out_weight):
    highest = lax.Precision.HIGHEST
    tok_range = jnp.arange(TOKS).astype(jnp.int32)[:, None]
    elapsed = (step_now[0] - last_step).astype(jnp.float32)
    factor = jnp.exp(elapsed * decay_log)
    group_of = (jnp.arange(SAMPLES).astype(jnp.int32) // BATCH)[None, :]
    owner = sample_slots // CAP
    within = sample_slots % CAP
    local_id = row_ids[tok_range, owner, group_of, within]
    global_id = (owner * ROWS_DEV + local_id).astype(jnp.int32)
    own_rows = row_table[tok_range, global_id] * factor[tok_range, global_id][:, :, None]
    mixed_rows = swap_heads(own_rows)
    normed_in, inverse_in = normalize(own_rows + mixed_rows)
    input_bf = normed_in.astype(jnp.bfloat16)
    up_full = up_weight.astype(jnp.float32)
    down_full = down_weight.astype(jnp.float32)
    preact = jnp.einsum('tsd,dtf->tsf', input_bf.astype(jnp.float32), up_full, precision=highest)
    active = jax.nn.gelu(preact, approximate=False).astype(jnp.bfloat16)
    output = jnp.einsum('tsf,dtf->tsd', active.astype(jnp.float32), down_full, precision=highest)
    normed_out, inverse_out = normalize(normed_in + output)
    logits = jnp.einsum('tsd,td->s', normed_out, out_weight, precision=highest)
    dlogit = jax.nn.sigmoid(logits) - labels.astype(jnp.float32)
    grad_norm_out = dlogit[None, :, None] * out_weight[:, None, :]
    grad_sum = norm_back(grad_norm_out, normed_out, inverse_out)
    grad_out_bf = grad_sum.astype(jnp.bfloat16)
    grad_active = jnp.einsum('tsd,dtf->tsf', grad_out_bf.astype(jnp.float32), down_full, precision=highest)
    grad_pre = (grad_active * gelu_grad(preact)).astype(jnp.bfloat16)
    grad_normed = grad_sum + jnp.einsum('tsf,dtf->tsd', grad_pre.astype(jnp.float32), up_full, precision=highest)
    grad_mixed = norm_back(grad_normed, normed_in, inverse_in)
    grad_rows_all = grad_mixed + swap_heads(grad_mixed)
    row_grads = jnp.zeros((TOKS, ROWS, D), jnp.float32).at[tok_range, global_id].add(grad_rows_all)
    tok_four = jnp.arange(TOKS).astype(jnp.int32)[:, None, None, None]
    valid_slot = (jnp.arange(CAP).astype(jnp.int32)[None, None, None, :] < row_counts[:, :, :, None]).astype(jnp.float32)
    list_global = (jnp.arange(N_SMP).astype(jnp.int32)[None, :, None, None] * ROWS_DEV + row_ids).astype(jnp.int32)
    hits = jnp.zeros((TOKS, ROWS), jnp.float32).at[tok_four, list_global].add(valid_slot)
    touched = hits > 0.0
    new_accum = row_accum + lax.optimization_barrier(jnp.mean(row_grads * row_grads, axis=2))
    updated = row_table * factor[:, :, None] - learn_rate * row_grads * lax.rsqrt(new_accum)[:, :, None]
    new_table = jnp.where(touched[:, :, None], updated, row_table)
    grad_down = jnp.einsum('tsd,tsf->dtf', grad_out_bf.astype(jnp.float32), active.astype(jnp.float32), precision=highest)
    return (new_table, new_accum, grad_down, logits)
```

```python
import math

import jax
import jax.numpy as jnp
import numpy as np
from jax import lax
from jax.experimental import pallas as pl
from jax.experimental.pallas import tpu as pltpu
from jax.sharding import Mesh
from jax.sharding import PartitionSpec as P

decay_log = math.log(0.98)
learn_rate = 0.2
norm_eps = 1e-05
f32 = jnp.float32
bf16 = jnp.bfloat16
f16 = jnp.float16
i32 = jnp.int32


NN = (((1,), (0,)), ((), ()))
NT = (((1,), (1,)), ((), ()))
VM = pl.BlockSpec(memory_space=pltpu.VMEM)
SM = pl.BlockSpec(memory_space=pltpu.SMEM)


def dot(a, b, dims=NN):
    return lax.dot_general(a, b, dims, preferred_element_type=f32)


def split(v):
    hi = v.astype(bf16)
    return hi, (v - hi.astype(f32)).astype(bf16)


def dot2(v, b, dims=NN):
    hi, lo = split(v)
    return dot(hi, b, dims) + dot(lo, b, dims)


def iota(shape, dim):
    return lax.broadcasted_iota(i32, shape, dim)


def call(body, outs, name, scratch=(), n_in=0, smem=0, flops=0, nbytes=0):
    return pl.pallas_call(
        body,
        out_shape=outs,
        in_specs=[SM] * smem + [VM] * (n_in - smem),
        out_specs=jax.tree.map(lambda _: VM, outs),
        scratch_shapes=list(scratch),
        compiler_params=pltpu.CompilerParams(vmem_limit_bytes=40 * 2**20),
        cost_estimate=pl.CostEstimate(flops=flops, bytes_accessed=nbytes, transcendentals=0),
        name=name,
    )


def sds(shape, dtype=f32):
    return jax.ShapeDtypeStruct(shape, dtype)


def slot_columns(tab, cols, chips):
    groups = tab.shape[1]
    col = iota((1, cols), 1)
    chip, tok, grp, slot = col // 8, (col // 4) % 2, (col // 2) % 2, col % 2
    pick = (iota((groups, cols), 0) == chip * 2 + grp).astype(f32)
    every = lax.dot_general(tab, pick, NN, preferred_element_type=f32, precision=lax.Precision.HIGHEST)
    keep = iota((4, cols), 0) == tok * 2 + slot
    return jnp.sum(jnp.where(keep, every, 0.0), axis=0, keepdims=True), tok, slot


def lookup_body(step_ref, table_ref, last_ref, ids_ref, out_ref):
    toks, rows, width = table_ref.shape
    cols = out_ref.shape[0]
    ids, tok, _ = slot_columns(ids_ref[...].astype(f32), cols, cols // 8)
    ids = ids + tok.astype(f32) * rows
    column = jnp.transpose(jnp.broadcast_to(ids, (8, cols)))[:, 0:1]
    total = jnp.zeros((cols, width), f32)
    for j in range(toks):
        elapsed = (step_ref[0] - last_ref[j : j + 1, :]).astype(f32)
        factor = jnp.exp(elapsed * decay_log)
        hit = iota((cols, rows), 1).astype(f32) + (j * rows) == column
        weights = jnp.where(hit, factor, 0.0)
        total = total + lax.dot_general(
            weights, table_ref[j], NN, preferred_element_type=f32, precision=lax.Precision.HIGHEST
        )
    out_ref[...] = total


def list_targets(slots, half):
    group = (iota(slots.shape, 1) >= half).astype(i32)
    return (slots // 2) * 4 + group * 2 + slots % 2


def own_target(targets, token):
    return jnp.sum(jnp.where(iota(targets.shape, 0) == token, targets, 0), axis=0, keepdims=True)


def forward_body(
    where_ref, own_ref, heads_ref, slots_ref, head_ref, order_ref,
    z_ref, xp_ref, xm_ref, xa_ref, xb_ref,
    normed_in_ref, inv_in_ref, active_ref, slope_ref, up_ref, down_ref, normed_out_ref, inv_out_ref, logit_ref,
    all_ref, total_ref, input_ref,
):
    width, lists = own_ref.shape
    samples = slots_ref.shape[1]
    toks = slots_ref.shape[0] // 2
    head = width // toks
    hidden = z_ref.shape[1]
    part = z_ref.shape[0]
    all_ref[0:part] = z_ref[...]
    all_ref[part : 2 * part] = xp_ref[...]
    all_ref[2 * part : 3 * part] = xm_ref[...]
    all_ref[3 * part : 3 * part + part // 2] = xa_ref[...]
    all_ref[3 * part + part // 2 : 4 * part] = xb_ref[...]
    targets = list_targets(slots_ref[0:toks, :], samples // 2)
    row = iota((lists, samples), 0)
    one_own = (row == own_target(targets, where_ref[0])).astype(bf16)
    own = dot2(own_ref[...], one_own)
    mixed = []
    for t in range(toks):
        one = (row == targets[t : t + 1, :]).astype(bf16)
        mixed.append(dot2(heads_ref[t * head : (t + 1) * head, :], one))
    value = own + jnp.concatenate(mixed, axis=0)
    centre = jnp.mean(value, axis=0, keepdims=True)
    shifted = value - centre
    inverse = lax.rsqrt(jnp.mean(shifted * shifted, axis=0, keepdims=True) + norm_eps)
    normed = shifted * inverse
    normed_in_ref[...] = normed
    inv_in_ref[...] = inverse
    input_ref[...] = jnp.transpose(normed.astype(bf16))
    total_ref[...] = jnp.zeros_like(total_ref)
    rows = all_ref.shape[0]
    order_up = (iota((width, rows), 0) == order_ref[0:1, :]).astype(bf16)
    order_down = (iota((width, rows), 0) == order_ref[1:2, :]).astype(bf16)
    chunk = 256

    @pl.loop(0, hidden // chunk)
    def _(i):
        cols = pl.ds(pl.multiple_of(i * chunk, chunk), chunk)
        block = all_ref[:, cols]
        up = dot(order_up, block).astype(bf16)
        down = dot(order_down, block).astype(bf16)
        up_ref[:, cols] = up
        down_ref[:, cols] = down
        pre = dot(input_ref[...], up)
        cumulative = 0.5 * (1.0 + lax.erf(pre * (1.0 / math.sqrt(2.0))))
        density = jnp.exp(-0.5 * pre * pre) * (1.0 / math.sqrt(2.0 * math.pi))
        active = (pre * cumulative).astype(bf16)
        active_ref[:, cols] = active
        slope_ref[:, cols] = cumulative + pre * density
        total_ref[...] += dot(down, active, NT)

    value = normed_in_ref[...] + total_ref[...]
    centre = jnp.mean(value, axis=0, keepdims=True)
    shifted = value - centre
    inverse = lax.rsqrt(jnp.mean(shifted * shifted, axis=0, keepdims=True) + norm_eps)
    normed = shifted * inverse
    normed_out_ref[...] = normed
    inv_out_ref[...] = inverse
    logit_ref[...] = jnp.sum(normed * head_ref[...], axis=0, keepdims=True)


def norm_back(grad_in, normed, inverse):
    first = jnp.mean(grad_in, axis=0, keepdims=True)
    second = jnp.mean(grad_in * normed, axis=0, keepdims=True)
    return inverse * (grad_in - first - normed * second)


def grad_down_body(
    logit_ref, slots_ref, head_ref, normed_out_ref, inv_out_ref, active_ref,
    grad_sum_ref, grad_out_ref, grad_down_ref, padded_ref,
):
    toks = slots_ref.shape[0] // 2
    width = head_ref.shape[0]
    labels = slots_ref[toks : toks + 1, :].astype(f32)
    dlogit = jax.nn.sigmoid(logit_ref[...]) - labels
    grad = norm_back(dlogit * head_ref[...], normed_out_ref[...], inv_out_ref[...])
    grad_sum_ref[...] = grad
    rounded = grad.astype(bf16)
    grad_out_ref[...] = jnp.transpose(rounded)
    lines = padded_ref.shape[0]
    line = iota((lines, width), 0)
    source = (line // 16) * 12 + ((line % 16) // 8) * 6 + line % 8
    place = ((source == iota((lines, width), 1)) & (line % 8 < 6)).astype(bf16)
    padded_ref[...] = dot(place, rounded).astype(bf16)
    chunk = 256

    @pl.loop(0, active_ref.shape[1] // chunk)
    def _(i):
        cols = pl.ds(pl.multiple_of(i * chunk, chunk), chunk)
        grad_down_ref[:, cols] = dot(padded_ref[...], active_ref[:, cols]).astype(bf16)


def grad_rows_body(
    where_ref, slots_ref, grad_sum_ref, grad_out_ref, slope_ref, up_ref, down_ref, normed_in_ref, inv_in_ref,
    own_ref, back_ref, total_ref,
):
    width, lists = own_ref.shape
    samples = slots_ref.shape[1]
    toks = slots_ref.shape[0] // 2
    head = width // toks
    total_ref[...] = grad_sum_ref[...]
    chunk = 256

    @pl.loop(0, slope_ref.shape[1] // chunk)
    def _(i):
        cols = pl.ds(pl.multiple_of(i * chunk, chunk), chunk)
        grad = dot(grad_out_ref[...], down_ref[:, cols])
        grad_pre = (grad * slope_ref[:, cols]).astype(bf16)
        total_ref[...] += dot(up_ref[:, cols], grad_pre, NT)

    mixed = norm_back(total_ref[...], normed_in_ref[...], inv_in_ref[...])
    targets = list_targets(slots_ref[0:toks, :], samples // 2)
    row = iota((lists, samples), 0)
    one_own = (row == own_target(targets, where_ref[0])).astype(bf16)
    hi, lo = split(mixed)
    own_ref[...] = dot(hi, one_own, NT) + dot(lo, one_own, NT)
    for t in range(toks):
        one = (row == targets[t : t + 1, :]).astype(bf16)
        span = slice(t * head, (t + 1) * head)
        back_ref[span, :] = (dot(hi[span], one, NT) + dot(lo[span], one, NT)).astype(bf16)


def update_body(
    step_ref, table_ref, accum_ref, last_ref, ids_ref, counts_ref, back_ref,
    table_out_ref, accum_out_ref,
):
    toks, rows, width = table_ref.shape
    cols = back_ref.shape[0]
    ids, tok, slot = slot_columns(ids_ref[...].astype(f32), cols, cols // 8)
    counts = counts_ref[...].astype(f32)
    groups = counts.shape[1]
    four = jnp.concatenate([counts[0:1], counts[0:1], counts[1:2], counts[1:2]], axis=0)
    have, _, _ = slot_columns(four, cols, cols // 8)
    valid = slot.astype(f32) < have
    row = iota((rows, cols), 0).astype(f32)
    back = back_ref[...]
    for j in range(toks):
        named = jnp.where((tok == j) & valid, ids, -1.0)
        hit = (row == named).astype(f32)
        grads = dot(hit.astype(bf16), back)
        square = grads * grads
        touched = jnp.max(hit, axis=1, keepdims=True) > 0.0
        flat = jnp.concatenate(
            [last_ref[j : j + 1, :].astype(f32), accum_ref[j : j + 1, :], jnp.zeros((6, rows), f32)], axis=0
        )
        upright = jnp.transpose(flat)
        factor = jnp.exp((step_ref[0].astype(f32) - upright[:, 0:1]) * decay_log)
        accum = upright[:, 1:2] + jnp.mean(square, axis=1, keepdims=True)
        wide = jnp.transpose(jnp.broadcast_to(accum, (rows, 8)))
        accum_out_ref[j : j + 1, :] = wide[0:1, :]
        table = table_ref[j]
        updated = table * factor - learn_rate * grads * lax.rsqrt(accum)
        table_out_ref[j] = jnp.where(touched, updated, table)


def ring(value, axis, size, shift):
    return lax.ppermute(value, axis, [(i, (i + shift) % size) for i in range(size)])


def flip(value, axis, size, bit):
    return lax.ppermute(value, axis, [(i, i ^ bit) for i in range(size)])


def weight_order(x, z, core, n_x, n_z, steps_z, part):
    block = part // n_z
    third = block // 4
    line = np.arange(4 * part)
    section = line // part
    step_x = np.array([0, -1, 1, 2])[section]
    step_z = np.asarray(steps_z)[(line % part) // block]
    inner = line % block
    other = inner // (2 * third)
    is_down = (inner // third) % 2
    r = inner % third
    chip = ((x + step_x + n_x) % n_x) * n_z + (z + step_z + n_z) % n_z
    owner = jnp.where(core == 0, other, 1 - other)
    target = (chip * 2 + owner) * third + r
    return jnp.stack([jnp.where(is_down == 0, target, -1), jnp.where(is_down == 1, target, -1)]).astype(i32)


def on_device(
    row_table, row_accum, last_step, step_now, row_ids, row_counts, sample_slots, labels, up_weight, down_weight, out_weight
):
    n_tok, n_x, n_z = lax.axis_size("tok"), lax.axis_size("x"), lax.axis_size("z")
    local_toks, shard_rows, width = row_table.shape
    toks, batch = sample_slots.shape
    groups, capacity = row_ids.shape[2:]
    head = width // toks
    hidden = up_weight.shape[2]
    lists = 2 * groups * capacity
    samples = 2 * batch
    core = lax.axis_index("core")
    token = lax.axis_index("tok") * 2 + core

    ids = row_ids[:, 0].transpose(0, 2, 1).reshape(2 * capacity, groups)
    looked = call(
        lookup_body, sds((lists, width)), "lookup", n_in=4, smem=1, flops=10**9, nbytes=2 * 10**6
    )(step_now, row_table, last_step, ids)
    sent = looked.astype(f16).reshape(groups, 2 * capacity, width)
    got = lax.all_to_all(sent, ("x", "z", "core"), 0, 0, tiled=True)
    own = got.reshape(lists, width).T
    heads = lax.all_to_all(own.reshape(toks, head, lists), ("tok", "core"), 0, 0, tiled=True)
    heads = heads.reshape(width, lists).astype(f32)
    own = own.astype(f32)

    mine = jnp.concatenate([sample_slots, labels[None], jnp.zeros((toks - 1, batch), i32)], axis=0)
    theirs = flip(mine, "core", 2, 1)
    slots = jnp.where(core == 0, jnp.concatenate([mine, theirs], axis=1), jnp.concatenate([theirs, mine], axis=1))

    both = jnp.concatenate([up_weight, down_weight], axis=0)
    keep = jnp.where(core == 0, both[:, 0], both[:, 1])
    give = jnp.where(core == 0, both[:, 1], both[:, 0])
    piece = jnp.concatenate([keep, flip(give, "core", 2, 1)], axis=0)
    before, after = ring(piece, "z", n_z, 1), ring(piece, "z", n_z, -1)
    pair = jnp.concatenate([before, piece], axis=0)
    three = jnp.concatenate([before, piece, after], axis=0)
    line = jnp.concatenate([three, ring(three, "z", n_z, 3), ring(pair, "z", n_z, -3)], axis=0)
    steps_z = (-1, 0, 1, -4, -3, -2, 2, 3)
    part = line.shape[0]
    x_before, x_after = ring(line, "x", n_x, 1), ring(line, "x", n_x, -1)
    far_a = ring(x_before[: part // 2], "x", n_x, 1)
    far_b = ring(x_after[part // 2 :], "x", n_x, -1)
    order = weight_order(lax.axis_index("x"), lax.axis_index("z"), core, n_x, n_z, steps_z, part)

    where = token.reshape(1).astype(i32)
    head_weight = jnp.where(core == 0, out_weight[0], out_weight[1])[:, None]
    full = (samples, hidden)
    normed_in, inv_in, active, slope, up, down, normed_out, inv_out, partial = call(
        forward_body,
        (
            sds((width, samples)), sds((1, samples)), sds(full, bf16), sds(full), sds((width, hidden), bf16),
            sds((width, hidden), bf16), sds((width, samples)), sds((1, samples)), sds((1, samples)),
        ),
        "forward",
        scratch=(
            pltpu.VMEM((4 * part, hidden), bf16), pltpu.VMEM((width, samples), f32), pltpu.VMEM((samples, width), bf16)
        ),
        n_in=11, smem=1, flops=4 * 10**9, nbytes=10**7,
    )(where, own, heads, slots, head_weight, order, line, x_before, x_after, far_a, far_b)
    logits = partial + flip(partial, "core", 2, 1)
    logits = logits + flip(logits, "tok", n_tok, 1)
    logits = logits + flip(logits, "tok", n_tok, 2)

    lines = n_x * n_z * 16
    grad_sum, grad_out, grad_down = call(
        grad_down_body,
        (sds((width, samples)), sds((samples, width), bf16), sds((lines, hidden), bf16)),
        "grad_down",
        scratch=(pltpu.VMEM((lines, samples), bf16),),
        n_in=6, flops=10**9, nbytes=4 * 10**6,
    )(logits, slots, head_weight, normed_out, inv_out, active)
    parts = lax.all_to_all(grad_down.reshape(n_x * n_z, 16, hidden), ("x", "z"), 0, 0, tiled=True)

    own_grads, head_grads = call(
        grad_rows_body,
        (sds((width, lists)), sds((width, lists), bf16)),
        "grad_rows",
        scratch=(pltpu.VMEM((width, samples), f32),),
        n_in=9, smem=1, flops=2 * 10**9, nbytes=8 * 10**6,
    )(where, slots, grad_sum, grad_out, slope, up, down, normed_in, inv_in)
    returned = lax.all_to_all(head_grads.reshape(toks, head, lists), ("tok", "core"), 0, 0, tiled=True)
    list_grads = (own_grads + returned.reshape(width, lists).astype(f32)).T.astype(bf16)
    back = lax.all_to_all(list_grads.reshape(groups, 2 * capacity, width), ("x", "z", "core"), 0, 0, tiled=True)
    new_table, new_accum = call(
        update_body,
        (sds(row_table.shape), sds(row_accum.shape)),
        "update",
        n_in=7, smem=1, flops=10**9, nbytes=3 * 10**6,
    )(step_now, row_table, row_accum, last_step, ids, row_counts[:, 0], back.reshape(lists, width))

    summed = jnp.sum(parts.astype(f32), axis=0)
    third = width // (n_x * n_z * 2)
    low, high = summed[0:third], summed[8 : 8 + third]
    stay, leave = jnp.where(core == 0, low, high), jnp.where(core == 0, high, low)
    come = flip(leave, "core", 2, 1)
    grad_down = jnp.where(core == 0, jnp.stack([stay, come], axis=1), jnp.stack([come, stay], axis=1))
    logits = jnp.where(core == 0, logits[0, :batch], logits[0, batch:])
    return (new_table, new_accum, grad_down, logits)


def solution(mesh):
    devices = mesh.devices.reshape(4, 4, 8, 2)
    wide = Mesh(devices, ("tok", "x", "z", "core"))
    smp = ("x", "z", "core")
    return jax.shard_map(
        on_device,
        mesh=wide,
        in_specs=(
            P("tok", smp, None),
            P("tok", smp),
            P("tok", smp),
            P(),
            P("tok", smp, None, None),
            P("tok", smp, None),
            P(None, smp),
            P(smp),
            P(smp, "tok", None),
            P(smp, "tok", None),
            P("tok", None),
        ),
        out_specs=(P("tok", smp, None), P("tok", smp), P(smp, "tok", None), P(smp)),
        check_vma=False,
    )
```

```python
import math

import jax
import jax.numpy as jnp
import numpy as np
from jax import lax
from jax.experimental import pallas as pl
from jax.experimental.pallas import tpu as pltpu
from jax.sharding import Mesh
from jax.sharding import PartitionSpec as P


decay_log = math.log(0.98)
learn_rate = 0.2
norm_eps = 1e-05
f32 = jnp.float32
bf16 = jnp.bfloat16
f16 = jnp.float16
i32 = jnp.int32


NN = (((1,), (0,)), ((), ()))
NT = (((1,), (1,)), ((), ()))
VM = pl.BlockSpec(memory_space=pltpu.VMEM)
SM = pl.BlockSpec(memory_space=pltpu.SMEM)


def dot(a, b, dims=NN):
    return lax.dot_general(a, b, dims, preferred_element_type=f32)


def split(v):
    hi = v.astype(bf16)
    return hi, (v - hi.astype(f32)).astype(bf16)


def dot2(v, b, dims=NN):
    hi, lo = split(v)
    return dot(hi, b, dims) + dot(lo, b, dims)


def iota(shape, dim):
    return lax.broadcasted_iota(i32, shape, dim)


def call(body, outs, scratch=(), n_in=0, smem=0, flops=0, nbytes=0):
    return pl.pallas_call(
        body,
        out_shape=outs,
        in_specs=[SM] * smem + [VM] * (n_in - smem),
        out_specs=jax.tree.map(lambda _: VM, outs),
        scratch_shapes=list(scratch),
        compiler_params=pltpu.CompilerParams(vmem_limit_bytes=40 * 2**20),
        cost_estimate=pl.CostEstimate(flops=flops, bytes_accessed=nbytes, transcendentals=0),
    )


def sds(shape, dtype=f32):
    return jax.ShapeDtypeStruct(shape, dtype)


def slot_columns(tab, cols):
    groups = tab.shape[1]
    col = iota((1, cols), 1)
    chip, tok, grp, slot = col // 8, (col // 4) % 2, (col // 2) % 2, col % 2
    pick = (iota((groups, cols), 0) == chip * 2 + grp).astype(f32)
    every = lax.dot_general(tab, pick, NN, preferred_element_type=f32, precision=lax.Precision.HIGHEST)
    keep = iota((4, cols), 0) == tok * 2 + slot
    return jnp.sum(jnp.where(keep, every, 0.0), axis=0, keepdims=True), tok, slot


def lookup_body(step_ref, table_ref, last_ref, ids_ref, out_ref):
    toks, rows, width = table_ref.shape
    cols = out_ref.shape[0]
    ids, tok, _ = slot_columns(ids_ref[...].astype(f32), cols)
    ids = ids + tok.astype(f32) * rows
    column = jnp.transpose(jnp.broadcast_to(ids, (8, cols)))[:, 0:1]
    total = jnp.zeros((cols, width), f32)
    for j in range(toks):
        elapsed = (step_ref[0] - last_ref[j : j + 1, :]).astype(f32)
        factor = jnp.exp(elapsed * decay_log)
        hit = iota((cols, rows), 1).astype(f32) + (j * rows) == column
        weights = jnp.where(hit, factor, 0.0)
        total = total + lax.dot_general(
            weights, table_ref[j], NN, preferred_element_type=f32, precision=lax.Precision.HIGHEST
        )
    out_ref[...] = total


def list_targets(slots, half):
    group = (iota(slots.shape, 1) >= half).astype(i32)
    return (slots // 2) * 4 + group * 2 + slots % 2


def own_target(targets, token):
    return jnp.sum(jnp.where(iota(targets.shape, 0) == token, targets, 0), axis=0, keepdims=True)


def forward_body(
    where_ref, own_ref, heads_ref, slots_ref, head_ref, order_ref,
    z_ref, xp_ref, xm_ref, xa_ref, xb_ref,
    normed_in_ref, inv_in_ref, active_ref, slope_ref, up_ref, down_ref, normed_out_ref, inv_out_ref, logit_ref,
    all_ref, total_ref, input_ref,
):
    width, lists = own_ref.shape
    samples = slots_ref.shape[1]
    toks = slots_ref.shape[0] // 2
    head = width // toks
    hidden = z_ref.shape[1]
    part = z_ref.shape[0]
    all_ref[0:part] = z_ref[...]
    all_ref[part : 2 * part] = xp_ref[...]
    all_ref[2 * part : 3 * part] = xm_ref[...]
    all_ref[3 * part : 3 * part + part // 2] = xa_ref[...]
    all_ref[3 * part + part // 2 : 4 * part] = xb_ref[...]
    targets = list_targets(slots_ref[0:toks, :], samples // 2)
    row = iota((lists, samples), 0)
    one_own = (row == own_target(targets, where_ref[0])).astype(bf16)
    own = dot2(own_ref[...], one_own)
    mixed = []
    for t in range(toks):
        one = (row == targets[t : t + 1, :]).astype(bf16)
        mixed.append(dot2(heads_ref[t * head : (t + 1) * head, :], one))
    value = own + jnp.concatenate(mixed, axis=0)
    centre = jnp.mean(value, axis=0, keepdims=True)
    shifted = value - centre
    inverse = lax.rsqrt(jnp.mean(shifted * shifted, axis=0, keepdims=True) + norm_eps)
    normed = shifted * inverse
    normed_in_ref[...] = normed
    inv_in_ref[...] = inverse
    input_ref[...] = jnp.transpose(normed.astype(bf16))
    total_ref[...] = jnp.zeros_like(total_ref)
    rows = all_ref.shape[0]
    order_up = (iota((width, rows), 0) == order_ref[0:1, :]).astype(bf16)
    order_down = (iota((width, rows), 0) == order_ref[1:2, :]).astype(bf16)
    chunk = 256

    @pl.loop(0, hidden // chunk)
    def _(i):
        cols = pl.ds(pl.multiple_of(i * chunk, chunk), chunk)
        block = all_ref[:, cols]
        up = dot(order_up, block).astype(bf16)
        down = dot(order_down, block).astype(bf16)
        up_ref[:, cols] = up
        down_ref[:, cols] = down
        pre = dot(input_ref[...], up)
        cumulative = 0.5 * (1.0 + lax.erf(pre * (1.0 / math.sqrt(2.0))))
        density = jnp.exp(-0.5 * pre * pre) * (1.0 / math.sqrt(2.0 * math.pi))
        active = (pre * cumulative).astype(bf16)
        active_ref[:, cols] = active
        slope_ref[:, cols] = cumulative + pre * density
        total_ref[...] += dot(down, active, NT)

    value = normed_in_ref[...] + total_ref[...]
    centre = jnp.mean(value, axis=0, keepdims=True)
    shifted = value - centre
    inverse = lax.rsqrt(jnp.mean(shifted * shifted, axis=0, keepdims=True) + norm_eps)
    normed = shifted * inverse
    normed_out_ref[...] = normed
    inv_out_ref[...] = inverse
    logit_ref[...] = jnp.sum(normed * head_ref[...], axis=0, keepdims=True)


def norm_back(grad_in, normed, inverse):
    first = jnp.mean(grad_in, axis=0, keepdims=True)
    second = jnp.mean(grad_in * normed, axis=0, keepdims=True)
    return inverse * (grad_in - first - normed * second)


def grad_down_body(
    chip_ref, logit_ref, slots_ref, head_ref, normed_out_ref, inv_out_ref, active_ref,
    grad_sum_ref, grad_out_ref, kept_ref, next_ref, far_ref, last_ref, padded_ref,
):
    toks = slots_ref.shape[0] // 2
    width = head_ref.shape[0]
    labels = slots_ref[toks : toks + 1, :].astype(f32)
    dlogit = jax.nn.sigmoid(logit_ref[...]) - labels
    grad = norm_back(dlogit * head_ref[...], normed_out_ref[...], inv_out_ref[...])
    grad_sum_ref[...] = grad
    rounded = grad.astype(bf16)
    grad_out_ref[...] = jnp.transpose(rounded)
    lines, half = kept_ref.shape
    n_z = lines // 24
    line = iota((4 * lines, width), 0)
    chip_x = chip_ref[0] + line // lines
    chip_z = chip_ref[1] + line % lines // 24
    chip = chip_x % 4 * n_z + chip_z % n_z
    for k in range(2):
        source = chip * 12 + line % 24 - 12 * k
        place = (source == iota((4 * lines, width), 1)) & (line % 24 // 12 == k)
        padded_ref[k] = dot(place.astype(bf16), rounded).astype(bf16)
    chunk = 256

    @pl.loop(0, half // chunk)
    def _(i):
        cols = pl.ds(pl.multiple_of(i * chunk, chunk), chunk)
        more = pl.ds(pl.multiple_of(half + i * chunk, chunk), chunk)
        value = dot(padded_ref[0], active_ref[:, cols]) + dot(padded_ref[1], active_ref[:, more])
        kept_ref[:, cols] = value[0:lines]
        next_ref[:, cols] = value[lines : 2 * lines].astype(bf16)
        far_ref[:, cols] = value[2 * lines : 3 * lines].astype(bf16)
        last_ref[:, cols] = value[3 * lines :].astype(bf16)


def grad_rows_body(
    where_ref, slots_ref, grad_sum_ref, grad_out_ref, slope_ref, up_ref, down_ref, normed_in_ref, inv_in_ref,
    own_ref, back_ref, total_ref,
):
    width, lists = own_ref.shape
    samples = slots_ref.shape[1]
    toks = slots_ref.shape[0] // 2
    head = width // toks
    total_ref[...] = grad_sum_ref[...]
    chunk = 256

    @pl.loop(0, slope_ref.shape[1] // chunk)
    def _(i):
        cols = pl.ds(pl.multiple_of(i * chunk, chunk), chunk)
        grad = dot(grad_out_ref[...], down_ref[:, cols])
        grad_pre = (grad * slope_ref[:, cols]).astype(bf16)
        total_ref[...] += dot(up_ref[:, cols], grad_pre, NT)

    mixed = norm_back(total_ref[...], normed_in_ref[...], inv_in_ref[...])
    targets = list_targets(slots_ref[0:toks, :], samples // 2)
    row = iota((lists, samples), 0)
    one_own = (row == own_target(targets, where_ref[0])).astype(bf16)
    hi, lo = split(mixed)
    own_ref[...] = dot(hi, one_own, NT) + dot(lo, one_own, NT)
    for t in range(toks):
        one = (row == targets[t : t + 1, :]).astype(bf16)
        span = slice(t * head, (t + 1) * head)
        back_ref[span, :] = (dot(hi[span], one, NT) + dot(lo[span], one, NT)).astype(bf16)


def update_body(
    step_ref, table_ref, accum_ref, last_ref, ids_ref, counts_ref, back_ref,
    table_out_ref, accum_out_ref,
):
    toks, rows, _ = table_ref.shape
    cols = back_ref.shape[0]
    ids, tok, slot = slot_columns(ids_ref[...].astype(f32), cols)
    counts = counts_ref[...].astype(f32)
    four = jnp.concatenate([counts[0:1], counts[0:1], counts[1:2], counts[1:2]], axis=0)
    have, _, _ = slot_columns(four, cols)
    valid = slot.astype(f32) < have
    row = iota((rows, cols), 0).astype(f32)
    back = back_ref[...]
    for j in range(toks):
        named = jnp.where((tok == j) & valid, ids, -1.0)
        hit = (row == named).astype(f32)
        grads = dot(hit.astype(bf16), back)
        square = grads * grads
        touched = jnp.max(hit, axis=1, keepdims=True) > 0.0
        flat = jnp.concatenate(
            [last_ref[j : j + 1, :].astype(f32), accum_ref[j : j + 1, :], jnp.zeros((6, rows), f32)], axis=0
        )
        upright = jnp.transpose(flat)
        factor = jnp.exp((step_ref[0].astype(f32) - upright[:, 0:1]) * decay_log)
        accum = upright[:, 1:2] + jnp.mean(square, axis=1, keepdims=True)
        wide = jnp.transpose(jnp.broadcast_to(accum, (rows, 8)))
        accum_out_ref[j : j + 1, :] = wide[0:1, :]
        table = table_ref[j]
        updated = table * factor - learn_rate * grads * lax.rsqrt(accum)
        table_out_ref[j] = jnp.where(touched, updated, table)


def ring(value, axis, size, shift):
    return lax.ppermute(value, axis, [(i, (i + shift) % size) for i in range(size)])


def flip(value, axis, size, bit):
    return lax.ppermute(value, axis, [(i, i ^ bit) for i in range(size)])


def weight_order(x, z, core, n_x, n_z, steps_z, part):
    block = part // n_z
    third = block // 4
    line = np.arange(4 * part)
    section = line // part
    step_x = np.array([0, -1, 1, 2])[section]
    step_z = np.asarray(steps_z)[(line % part) // block]
    inner = line % block
    other = inner // (2 * third)
    is_down = (inner // third) % 2
    r = inner % third
    chip = ((x + step_x + n_x) % n_x) * n_z + (z + step_z + n_z) % n_z
    owner = jnp.where(core == 0, other, 1 - other)
    target = (chip * 2 + owner) * third + r
    return jnp.stack([jnp.where(is_down == 0, target, -1), jnp.where(is_down == 1, target, -1)]).astype(i32)


def on_device(
    row_table, row_accum, last_step, step_now, row_ids, row_counts, sample_slots, labels, up_weight, down_weight, out_weight
):
    n_tok, n_x, n_z = lax.axis_size("tok"), lax.axis_size("x"), lax.axis_size("z")
    _, _, width = row_table.shape
    toks, batch = sample_slots.shape
    groups, capacity = row_ids.shape[2:]
    head = width // toks
    hidden = up_weight.shape[2]
    lists = 2 * groups * capacity
    samples = 2 * batch
    core = lax.axis_index("core")
    token = lax.axis_index("tok") * 2 + core

    ids = row_ids[:, 0].transpose(0, 2, 1).reshape(2 * capacity, groups)
    looked = call(
        lookup_body, sds((lists, width)), n_in=4, smem=1, flops=10**9, nbytes=2 * 10**6
    )(step_now, row_table, last_step, ids)
    sent = looked.astype(f16).reshape(groups, 2 * capacity, width)
    got = lax.all_to_all(sent, ("x", "z", "core"), 0, 0, tiled=True)
    own = got.reshape(lists, width).T
    heads = lax.all_to_all(own.reshape(toks, head, lists), ("tok", "core"), 0, 0, tiled=True)
    heads = heads.reshape(width, lists).astype(f32)
    own = own.astype(f32)

    mine = jnp.concatenate([sample_slots, labels[None], jnp.zeros((toks - 1, batch), i32)], axis=0)
    theirs = flip(mine, "core", 2, 1)
    slots = jnp.where(core == 0, jnp.concatenate([mine, theirs], axis=1), jnp.concatenate([theirs, mine], axis=1))

    both = jnp.concatenate([up_weight, down_weight], axis=0)
    keep = jnp.where(core == 0, both[:, 0], both[:, 1])
    give = jnp.where(core == 0, both[:, 1], both[:, 0])
    piece = jnp.concatenate([keep, flip(give, "core", 2, 1)], axis=0)
    before, after = ring(piece, "z", n_z, 1), ring(piece, "z", n_z, -1)
    pair = jnp.concatenate([before, piece], axis=0)
    three = jnp.concatenate([before, piece, after], axis=0)
    far_before, far_after = ring(three, "z", n_z, 3), ring(pair, "z", n_z, -3)
    line = jnp.concatenate([three, far_before, far_after], axis=0)
    steps_z = (-1, 0, 1, -4, -3, -2, 2, 3)
    part = line.shape[0]
    x_before, x_after = ring(line, "x", n_x, 1), ring(line, "x", n_x, -1)
    far_a = ring(x_before[: part // 2], "x", n_x, 1)
    far_b = ring(x_after[part // 2 :], "x", n_x, -1)
    order = weight_order(lax.axis_index("x"), lax.axis_index("z"), core, n_x, n_z, steps_z, part)

    where = token.reshape(1).astype(i32)
    head_weight = jnp.where(core == 0, out_weight[0], out_weight[1])[:, None]
    full = (samples, hidden)
    normed_in, inv_in, active, slope, up, down, normed_out, inv_out, partial = call(
        forward_body,
        (
            sds((width, samples)), sds((1, samples)), sds(full, bf16), sds(full), sds((width, hidden), bf16),
            sds((width, hidden), bf16), sds((width, samples)), sds((1, samples)), sds((1, samples)),
        ),
        scratch=(
            pltpu.VMEM((4 * part, hidden), bf16), pltpu.VMEM((width, samples), f32), pltpu.VMEM((samples, width), bf16)
        ),
        n_in=11, smem=1, flops=4 * 10**9, nbytes=10**7,
    )(where, own, heads, slots, head_weight, order, line, x_before, x_after, far_a, far_b)
    logits = partial + flip(partial, "core", 2, 1)
    there = [flip(logits, "tok", n_tok, k) for k in (1, 2, 3)]
    logits = (logits + there[0]) + (there[1] + there[2])

    third = width // (n_x * n_z * 2)
    lines = n_z * 4 * third
    block = (lines, hidden // 2)
    chip = jnp.stack([lax.axis_index("x"), lax.axis_index("z")]).astype(i32)
    grad_sum, grad_out, kept, *away = call(
        grad_down_body,
        (sds((width, samples)), sds((samples, width), bf16), sds(block), sds(block, bf16), sds(block, bf16), sds(block, bf16)),
        scratch=(pltpu.VMEM((2, n_x * lines, samples), bf16),),
        n_in=7, smem=1, flops=10**9, nbytes=4 * 10**6,
    )(chip, logits, slots, head_weight, normed_out, inv_out, active)
    come = [ring(v, "x", n_x, k + 1) for k, v in enumerate(away)]
    total = kept + sum(v.astype(f32) for v in come)
    total = [total[k * 4 * third : (k + 1) * 4 * third] for k in range(n_z)]
    for k in range(1, n_z):
        total[k] = ring(total[k], "z", n_z, k)

    own_grads, head_grads = call(
        grad_rows_body,
        (sds((width, lists)), sds((width, lists), bf16)),
        scratch=(pltpu.VMEM((width, samples), f32),),
        n_in=9, smem=1, flops=2 * 10**9, nbytes=8 * 10**6,
    )(where, slots, grad_sum, grad_out, slope, up, down, normed_in, inv_in)
    returned = lax.all_to_all(head_grads.reshape(toks, head, lists), ("tok", "core"), 0, 0, tiled=True)
    list_grads = (own_grads + returned.reshape(width, lists).astype(f32)).T.astype(bf16)
    back = lax.all_to_all(list_grads.reshape(groups, 2 * capacity, width), ("x", "z", "core"), 0, 0, tiled=True)
    new_table, new_accum = call(
        update_body,
        (sds(row_table.shape), sds(row_accum.shape)),
        n_in=7, smem=1, flops=10**9, nbytes=3 * 10**6,
    )(step_now, row_table, row_accum, last_step, ids, row_counts[:, 0], back.reshape(lists, width))

    summed = sum(total[1:], total[0])
    summed = jnp.concatenate([summed[: 2 * third], summed[2 * third :]], axis=1)
    low, high = summed[:third], summed[third:]
    stay, leave = jnp.where(core == 0, low, high), jnp.where(core == 0, high, low)
    come = flip(leave, "core", 2, 1)
    grad_down = jnp.where(core == 0, jnp.stack([stay, come], axis=1), jnp.stack([come, stay], axis=1))
    logits = jnp.where(core == 0, logits[0, :batch], logits[0, batch:])
    return (new_table, new_accum, grad_down, logits)


def solution(mesh):
    devices = mesh.devices.reshape(4, 4, 8, 2)
    wide = Mesh(devices, ("tok", "x", "z", "core"))
    smp = ("x", "z", "core")
    return jax.shard_map(
        on_device,
        mesh=wide,
        in_specs=(
            P("tok", smp, None),
            P("tok", smp),
            P("tok", smp),
            P(),
            P("tok", smp, None, None),
            P("tok", smp, None),
            P(None, smp),
            P(smp),
            P(smp, "tok", None),
            P(smp, "tok", None),
            P("tok", None),
        ),
        out_specs=(P("tok", smp, None), P("tok", smp), P(smp, "tok", None), P(smp)),
        check_vma=False,
    )
```

```python
import math

import jax
import jax.numpy as jnp
import numpy as np
from jax import lax
from jax.experimental import pallas as pl
from jax.experimental.pallas import tpu as pltpu
from jax.sharding import Mesh
from jax.sharding import PartitionSpec as P


decay_log = math.log(0.98)
learn_rate = 0.2
norm_eps = 1e-05
f32 = jnp.float32
bf16 = jnp.bfloat16
f16 = jnp.float16
i32 = jnp.int32


NN = (((1,), (0,)), ((), ()))
NT = (((1,), (1,)), ((), ()))
VM = pl.BlockSpec(memory_space=pltpu.VMEM)
SM = pl.BlockSpec(memory_space=pltpu.SMEM)


def dot(a, b, dims=NN):
    return lax.dot_general(a, b, dims, preferred_element_type=f32)


def split(v):
    hi = v.astype(bf16)
    return hi, (v - hi.astype(f32)).astype(bf16)


def dot2(v, b, dims=NN):
    hi, lo = split(v)
    return dot(hi, b, dims) + dot(lo, b, dims)


def iota(shape, dim):
    return lax.broadcasted_iota(i32, shape, dim)


def call(body, outs, scratch=(), n_in=0, smem=0, flops=0, nbytes=0):
    return pl.pallas_call(
        body,
        out_shape=outs,
        in_specs=[SM] * smem + [VM] * (n_in - smem),
        out_specs=jax.tree.map(lambda _: VM, outs),
        scratch_shapes=list(scratch),
        compiler_params=pltpu.CompilerParams(vmem_limit_bytes=40 * 2**20),
        cost_estimate=pl.CostEstimate(flops=flops, bytes_accessed=nbytes, transcendentals=0),
    )


def sds(shape, dtype=f32):
    return jax.ShapeDtypeStruct(shape, dtype)


def slot_columns(tab, cols):
    groups = tab.shape[1]
    col = iota((1, cols), 1)
    chip, tok, grp, slot = col // 8, (col // 4) % 2, (col // 2) % 2, col % 2
    pick = (iota((groups, cols), 0) == chip * 2 + grp).astype(f32)
    every = lax.dot_general(tab, pick, NN, preferred_element_type=f32, precision=lax.Precision.HIGHEST)
    keep = iota((4, cols), 0) == tok * 2 + slot
    return jnp.sum(jnp.where(keep, every, 0.0), axis=0, keepdims=True), tok, slot


def lookup_body(step_ref, table_ref, last_ref, ids_ref, out_ref):
    toks, rows, width = table_ref.shape
    cols = out_ref.shape[0]
    ids, tok, _ = slot_columns(ids_ref[...].astype(f32), cols)
    ids = ids + tok.astype(f32) * rows
    column = jnp.transpose(jnp.broadcast_to(ids, (8, cols)))[:, 0:1]
    total = jnp.zeros((cols, width), f32)
    for j in range(toks):
        elapsed = (step_ref[0] - last_ref[j : j + 1, :]).astype(f32)
        factor = jnp.exp(elapsed * decay_log)
        hit = iota((cols, rows), 1).astype(f32) + (j * rows) == column
        weights = jnp.where(hit, factor, 0.0)
        total = total + lax.dot_general(
            weights, table_ref[j], NN, preferred_element_type=f32, precision=lax.Precision.HIGHEST
        )
    out_ref[...] = total


def list_targets(slots, half):
    group = (iota(slots.shape, 1) >= half).astype(i32)
    return (slots // 2) * 4 + group * 2 + slots % 2


def own_target(targets, token):
    return jnp.sum(jnp.where(iota(targets.shape, 0) == token, targets, 0), axis=0, keepdims=True)


def order_body(order_ref, chip_ref, z_ref, xa_ref, xb_ref, xc_ref, xd_ref, xe_ref, xf_ref, up_ref, down_ref, place_ref, all_ref):
    part = z_ref.shape[0]
    half = part // 2
    width, hidden = up_ref.shape
    all_ref[0:part] = z_ref[...]
    for k, ref in enumerate((xa_ref, xb_ref, xc_ref, xd_ref, xe_ref, xf_ref)):
        all_ref[part + k * half : part + (k + 1) * half] = ref[...]
    rows = all_ref.shape[0]
    order_up = (iota((width, rows), 0) == order_ref[0:1, :]).astype(bf16)
    order_down = (iota((width, rows), 0) == order_ref[1:2, :]).astype(bf16)
    chunk = 256

    @pl.loop(0, hidden // chunk)
    def _(i):
        cols = pl.ds(pl.multiple_of(i * chunk, chunk), chunk)
        block = all_ref[:, cols]
        up_ref[:, cols] = dot(order_up, block).astype(bf16)
        down_ref[:, cols] = dot(order_down, block).astype(bf16)

    lines = place_ref.shape[1] // 4
    line = iota((4 * lines, width), 0)
    pos = line % lines // 24
    chip_x = (chip_ref[0] + line // lines) % 4
    chip_z = chip_ref[1] ^ (pos // 2 + pos % 2 * 4)
    chip = chip_x * (lines // 24) + chip_z
    for k in range(2):
        source = chip * 12 + line % 24 - 12 * k
        place = (source == iota((4 * lines, width), 1)) & (line % 24 // 12 == k)
        place_ref[k] = place.astype(bf16)


def forward_body(
    where_ref, own_ref, heads_ref, slots_ref, head_ref, up_ref, down_ref,
    normed_in_ref, inv_in_ref, active_ref, slope_ref, normed_out_ref, inv_out_ref, logit_ref,
    total_ref, input_ref,
):
    width, lists = own_ref.shape
    samples = slots_ref.shape[1]
    toks = slots_ref.shape[0] // 2
    head = width // toks
    hidden = up_ref.shape[1]
    targets = list_targets(slots_ref[0:toks, :], samples // 2)
    row = iota((lists, samples), 0)
    one_own = (row == own_target(targets, where_ref[0])).astype(bf16)
    own = dot2(own_ref[...], one_own)
    mixed = []
    for t in range(toks):
        one = (row == targets[t : t + 1, :]).astype(bf16)
        mixed.append(dot2(heads_ref[t * head : (t + 1) * head, :], one))
    value = own + jnp.concatenate(mixed, axis=0)
    centre = jnp.mean(value, axis=0, keepdims=True)
    shifted = value - centre
    inverse = lax.rsqrt(jnp.mean(shifted * shifted, axis=0, keepdims=True) + norm_eps)
    normed = shifted * inverse
    normed_in_ref[...] = normed
    inv_in_ref[...] = inverse
    input_ref[...] = jnp.transpose(normed.astype(bf16))
    total_ref[...] = jnp.zeros_like(total_ref)
    chunk = 256

    @pl.loop(0, hidden // chunk)
    def _(i):
        cols = pl.ds(pl.multiple_of(i * chunk, chunk), chunk)
        pre = dot(input_ref[...], up_ref[:, cols])
        cumulative = 0.5 * (1.0 + lax.erf(pre * (1.0 / math.sqrt(2.0))))
        density = jnp.exp(-0.5 * pre * pre) * (1.0 / math.sqrt(2.0 * math.pi))
        active = (pre * cumulative).astype(bf16)
        active_ref[:, cols] = active
        slope_ref[:, cols] = cumulative + pre * density
        total_ref[...] += dot(down_ref[:, cols], active, NT)

    value = normed_in_ref[...] + total_ref[...]
    centre = jnp.mean(value, axis=0, keepdims=True)
    shifted = value - centre
    inverse = lax.rsqrt(jnp.mean(shifted * shifted, axis=0, keepdims=True) + norm_eps)
    normed = shifted * inverse
    normed_out_ref[...] = normed
    inv_out_ref[...] = inverse
    logit_ref[...] = jnp.sum(normed * head_ref[...], axis=0, keepdims=True)


def norm_back(grad_in, normed, inverse):
    first = jnp.mean(grad_in, axis=0, keepdims=True)
    second = jnp.mean(grad_in * normed, axis=0, keepdims=True)
    return inverse * (grad_in - first - normed * second)


def grad_down_body(
    place_ref, logit_ref, slots_ref, head_ref, normed_out_ref, inv_out_ref, active_ref,
    grad_sum_ref, grad_out_ref, kept_ref, next_ref, far_ref, last_ref, padded_ref,
):
    toks = slots_ref.shape[0] // 2
    labels = slots_ref[toks : toks + 1, :].astype(f32)
    dlogit = jax.nn.sigmoid(logit_ref[...]) - labels
    grad = norm_back(dlogit * head_ref[...], normed_out_ref[...], inv_out_ref[...])
    grad_sum_ref[...] = grad
    rounded = grad.astype(bf16)
    grad_out_ref[...] = jnp.transpose(rounded)
    lines, half = kept_ref.shape
    for k in range(2):
        padded_ref[k] = dot(place_ref[k], rounded).astype(bf16)
    chunk = 256

    @pl.loop(0, half // chunk)
    def _(i):
        cols = pl.ds(pl.multiple_of(i * chunk, chunk), chunk)
        more = pl.ds(pl.multiple_of(half + i * chunk, chunk), chunk)
        value = dot(padded_ref[0], active_ref[:, cols]) + dot(padded_ref[1], active_ref[:, more])
        kept_ref[:, cols] = value[0:lines]
        next_ref[:, cols] = value[lines : 2 * lines].astype(bf16)
        far_ref[:, cols] = value[2 * lines : 3 * lines].astype(bf16)
        last_ref[:, cols] = value[3 * lines :].astype(bf16)


def grad_rows_body(
    where_ref, slots_ref, grad_sum_ref, grad_out_ref, slope_ref, up_ref, down_ref, normed_in_ref, inv_in_ref,
    own_ref, back_ref, total_ref,
):
    width, lists = own_ref.shape
    samples = slots_ref.shape[1]
    toks = slots_ref.shape[0] // 2
    head = width // toks
    total_ref[...] = grad_sum_ref[...]
    chunk = 256

    @pl.loop(0, slope_ref.shape[1] // chunk)
    def _(i):
        cols = pl.ds(pl.multiple_of(i * chunk, chunk), chunk)
        grad = dot(grad_out_ref[...], down_ref[:, cols])
        grad_pre = (grad * slope_ref[:, cols]).astype(bf16)
        total_ref[...] += dot(up_ref[:, cols], grad_pre, NT)

    mixed = norm_back(total_ref[...], normed_in_ref[...], inv_in_ref[...])
    targets = list_targets(slots_ref[0:toks, :], samples // 2)
    row = iota((lists, samples), 0)
    one_own = (row == own_target(targets, where_ref[0])).astype(bf16)
    hi, lo = split(mixed)
    own_ref[...] = dot(hi, one_own, NT) + dot(lo, one_own, NT)
    for t in range(toks):
        one = (row == targets[t : t + 1, :]).astype(bf16)
        span = slice(t * head, (t + 1) * head)
        back_ref[span, :] = (dot(hi[span], one, NT) + dot(lo[span], one, NT)).astype(bf16)


def update_body(
    step_ref, table_ref, accum_ref, last_ref, ids_ref, counts_ref, back_ref,
    table_out_ref, accum_out_ref,
):
    toks, rows, _ = table_ref.shape
    cols = back_ref.shape[0]
    ids, tok, slot = slot_columns(ids_ref[...].astype(f32), cols)
    counts = counts_ref[...].astype(f32)
    four = jnp.concatenate([counts[0:1], counts[0:1], counts[1:2], counts[1:2]], axis=0)
    have, _, _ = slot_columns(four, cols)
    valid = slot.astype(f32) < have
    row = iota((rows, cols), 0).astype(f32)
    back = back_ref[...]
    for j in range(toks):
        named = jnp.where((tok == j) & valid, ids, -1.0)
        hit = (row == named).astype(f32)
        grads = dot(hit.astype(bf16), back)
        square = grads * grads
        touched = jnp.max(hit, axis=1, keepdims=True) > 0.0
        flat = jnp.concatenate(
            [last_ref[j : j + 1, :].astype(f32), accum_ref[j : j + 1, :], jnp.zeros((6, rows), f32)], axis=0
        )
        upright = jnp.transpose(flat)
        factor = jnp.exp((step_ref[0].astype(f32) - upright[:, 0:1]) * decay_log)
        accum = upright[:, 1:2] + jnp.mean(square, axis=1, keepdims=True)
        wide = jnp.transpose(jnp.broadcast_to(accum, (rows, 8)))
        accum_out_ref[j : j + 1, :] = wide[0:1, :]
        table = table_ref[j]
        updated = table * factor - learn_rate * grads * lax.rsqrt(accum)
        table_out_ref[j] = jnp.where(touched, updated, table)


def ring(value, axis, size, shift):
    return lax.ppermute(value, axis, [(i, (i + shift) % size) for i in range(size)])


def flip(value, axis, size, bit):
    return lax.ppermute(value, axis, [(i, i ^ bit) for i in range(size)])


def weight_order(x, z, core, n_x, n_z, steps_z, part):
    block = part // n_z
    third = block // 4
    line = np.arange(4 * part)
    section = np.maximum(line // (part // 2) - 1, 0)
    step_x = np.array([0, -1, -1, 1, 1, 2, 2])[section]
    step_z = np.asarray(steps_z)[(line % part) // block]
    inner = line % block
    other = inner // (2 * third)
    is_down = (inner // third) % 2
    r = inner % third
    chip = ((x + step_x + n_x) % n_x) * n_z + (z + step_z + n_z) % n_z
    owner = jnp.where(core == 0, other, 1 - other)
    target = (chip * 2 + owner) * third + r
    return jnp.stack([jnp.where(is_down == 0, target, -1), jnp.where(is_down == 1, target, -1)]).astype(i32)


def on_device(
    row_table, row_accum, last_step, step_now, row_ids, row_counts, sample_slots, labels, up_weight, down_weight, out_weight
):
    n_tok, n_x, n_z = lax.axis_size("tok"), lax.axis_size("x"), lax.axis_size("z")
    _, _, width = row_table.shape
    toks, batch = sample_slots.shape
    groups, capacity = row_ids.shape[2:]
    head = width // toks
    hidden = up_weight.shape[2]
    lists = 2 * groups * capacity
    samples = 2 * batch
    core = lax.axis_index("core")
    token = lax.axis_index("tok") * 2 + core

    ids = row_ids[:, 0].transpose(0, 2, 1).reshape(2 * capacity, groups)
    looked = call(
        lookup_body, sds((lists, width)), n_in=4, smem=1, flops=10**9, nbytes=2 * 10**6
    )(step_now, row_table, last_step, ids)
    sent = looked.astype(f16).reshape(groups, 2 * capacity, width)
    got = lax.all_to_all(sent, ("x", "z", "core"), 0, 0, tiled=True)
    own = got.reshape(lists, width).T
    heads = lax.all_to_all(own.reshape(toks, head, lists), ("tok", "core"), 0, 0, tiled=True)
    heads = heads.reshape(width, lists).astype(f32)
    own = own.astype(f32)

    mine = jnp.concatenate([sample_slots, labels[None], jnp.zeros((toks - 1, batch), i32)], axis=0)
    theirs = flip(mine, "core", 2, 1)
    slots = jnp.where(core == 0, jnp.concatenate([mine, theirs], axis=1), jnp.concatenate([theirs, mine], axis=1))

    both = jnp.concatenate([up_weight, down_weight], axis=0)
    keep = jnp.where(core == 0, both[:, 0], both[:, 1])
    give = jnp.where(core == 0, both[:, 1], both[:, 0])
    piece = jnp.concatenate([keep, flip(give, "core", 2, 1)], axis=0)
    before, after = ring(piece, "z", n_z, 1), ring(piece, "z", n_z, -1)
    pair = jnp.concatenate([before, piece], axis=0)
    three = jnp.concatenate([before, piece, after], axis=0)
    far_before, far_after = ring(three, "z", n_z, 3), ring(pair, "z", n_z, -3)
    line = jnp.concatenate([three, far_before, far_after], axis=0)
    steps_z = (-1, 0, 1, -4, -3, -2, 2, 3)
    part = line.shape[0]
    half = part // 2
    lower, upper = line[:half], line[half:]
    before_a, after_b = ring(lower, "x", n_x, 1), ring(upper, "x", n_x, -1)
    before_b, after_a = ring(upper, "x", n_x, 1), ring(lower, "x", n_x, -1)
    far_a, far_b = ring(before_a, "x", n_x, 1), ring(after_b, "x", n_x, -1)
    order = weight_order(lax.axis_index("x"), lax.axis_index("z"), core, n_x, n_z, steps_z, part)
    third = width // (n_x * n_z * 2)
    lines = n_z * 4 * third
    chip = jnp.stack([lax.axis_index("x"), lax.axis_index("z")]).astype(i32)
    up, down, place = pl.pallas_call(
        order_body,
        out_shape=(sds((width, hidden), bf16), sds((width, hidden), bf16), sds((2, n_x * lines, width), bf16)),
        in_specs=[VM, SM] + [VM] * 7,
        out_specs=(VM, VM, VM),
        scratch_shapes=[pltpu.VMEM((4 * part, hidden), bf16)],
        compiler_params=pltpu.CompilerParams(vmem_limit_bytes=40 * 2**20),
        cost_estimate=pl.CostEstimate(flops=2 * 10**9, bytes_accessed=8 * 10**6, transcendentals=0),
        name="order",
    )(order, chip, line, before_a, before_b, after_a, after_b, far_a, far_b)

    where = token.reshape(1).astype(i32)
    head_weight = jnp.where(core == 0, out_weight[0], out_weight[1])[:, None]
    full = (samples, hidden)
    normed_in, inv_in, active, slope, normed_out, inv_out, partial = call(
        forward_body,
        (
            sds((width, samples)), sds((1, samples)), sds(full, bf16), sds(full),
            sds((width, samples)), sds((1, samples)), sds((1, samples)),
        ),
        scratch=(pltpu.VMEM((width, samples), f32), pltpu.VMEM((samples, width), bf16)),
        n_in=7, smem=1, flops=3 * 10**9, nbytes=8 * 10**6,
    )(where, own, heads, slots, head_weight, up, down)
    logits = partial + flip(partial, "core", 2, 1)
    there = [flip(logits, "tok", n_tok, k) for k in (1, 2, 3)]
    logits = (logits + there[0]) + (there[1] + there[2])

    block = (lines, hidden // 2)
    grad_sum, grad_out, kept, *away = call(
        grad_down_body,
        (sds((width, samples)), sds((samples, width), bf16), sds(block), sds(block, bf16), sds(block, bf16), sds(block, bf16)),
        scratch=(pltpu.VMEM((2, n_x * lines, samples), bf16),),
        n_in=7, flops=2 * 10**9, nbytes=5 * 10**6,
    )(place, logits, slots, head_weight, normed_out, inv_out, active)
    come = [ring(v, "x", n_x, k + 1) for k, v in enumerate(away)]
    pair = 8 * third
    total = kept + sum(v.astype(f32) for v in come)
    total = [total[k * pair : (k + 1) * pair] for k in range(n_z // 2)]
    total[1:] = [flip(v, "z", n_z, k + 1) for k, v in enumerate(total[1:])]
    total = (total[0] + total[1]) + (total[2] + total[3])
    stay, leave = total[: pair // 2], total[pair // 2 :]
    summed = stay + flip(leave, "z", n_z, n_z // 2)

    own_grads, head_grads = call(
        grad_rows_body,
        (sds((width, lists)), sds((width, lists), bf16)),
        scratch=(pltpu.VMEM((width, samples), f32),),
        n_in=9, smem=1, flops=2 * 10**9, nbytes=8 * 10**6,
    )(where, slots, grad_sum, grad_out, slope, up, down, normed_in, inv_in)
    returned = lax.all_to_all(head_grads.reshape(toks, head, lists), ("tok", "core"), 0, 0, tiled=True)
    list_grads = (own_grads + returned.reshape(width, lists).astype(f32)).T.astype(bf16)
    back = lax.all_to_all(list_grads.reshape(groups, 2 * capacity, width), ("x", "z", "core"), 0, 0, tiled=True)
    new_table, new_accum = call(
        update_body,
        (sds(row_table.shape), sds(row_accum.shape)),
        n_in=7, smem=1, flops=10**9, nbytes=3 * 10**6,
    )(step_now, row_table, row_accum, last_step, ids, row_counts[:, 0], back.reshape(lists, width))

    summed = jnp.concatenate([summed[: 2 * third], summed[2 * third :]], axis=1)
    low, high = summed[:third], summed[third:]
    stay, leave = jnp.where(core == 0, low, high), jnp.where(core == 0, high, low)
    come = flip(leave, "core", 2, 1)
    grad_down = jnp.where(core == 0, jnp.stack([stay, come], axis=1), jnp.stack([come, stay], axis=1))
    logits = jnp.where(core == 0, logits[0, :batch], logits[0, batch:])
    return (new_table, new_accum, grad_down, logits)


def solution(mesh):
    devices = mesh.devices.reshape(4, 4, 8, 2)
    wide = Mesh(devices, ("tok", "x", "z", "core"))
    smp = ("x", "z", "core")
    return jax.shard_map(
        on_device,
        mesh=wide,
        in_specs=(
            P("tok", smp, None),
            P("tok", smp),
            P("tok", smp),
            P(),
            P("tok", smp, None, None),
            P("tok", smp, None),
            P(None, smp),
            P(smp),
            P(smp, "tok", None),
            P(smp, "tok", None),
            P("tok", None),
        ),
        out_specs=(P("tok", smp, None), P("tok", smp), P(smp, "tok", None), P(smp)),
        check_vma=False,
    )
```

```python
import math

import jax
import jax.numpy as jnp
import numpy as np
from jax import lax
from jax.experimental import pallas as pl
from jax.experimental.pallas import tpu as pltpu
from jax.sharding import Mesh
from jax.sharding import PartitionSpec as P


decay_log = math.log(0.98)
learn_rate = 0.2
norm_eps = 1e-05
f32 = jnp.float32
bf16 = jnp.bfloat16
f16 = jnp.float16
i32 = jnp.int32


NN = (((1,), (0,)), ((), ()))
NT = (((1,), (1,)), ((), ()))
VM = pl.BlockSpec(memory_space=pltpu.VMEM)
SM = pl.BlockSpec(memory_space=pltpu.SMEM)
ANY = pl.BlockSpec(memory_space=pl.ANY)
HBM = pl.BlockSpec(memory_space=pltpu.HBM)


def dot(a, b, dims=NN):
    return lax.dot_general(a, b, dims, preferred_element_type=f32)


def split(v):
    hi = v.astype(bf16)
    return hi, (v - hi.astype(f32)).astype(bf16)


def dot2(v, b, dims=NN):
    hi, lo = split(v)
    return dot(hi, b, dims) + dot(lo, b, dims)


def iota(shape, dim):
    return lax.broadcasted_iota(i32, shape, dim)


def call(body, outs, name, scratch=(), n_in=0, smem=0, flops=0, nbytes=0, room=8, away=0):
    return pl.pallas_call(
        body,
        out_shape=outs,
        in_specs=[SM] * smem + [HBM if name == "lookup" else ANY] * away + [VM] * (n_in - smem - away),
        out_specs=jax.tree.map(lambda _: VM, outs),
        scratch_shapes=list(scratch),
        compiler_params=pltpu.CompilerParams(vmem_limit_bytes=room * 2**20),
        cost_estimate=pl.CostEstimate(flops=flops, bytes_accessed=nbytes, transcendentals=0),
    )


def sds(shape, dtype=f32):
    return jax.ShapeDtypeStruct(shape, dtype)


def slot_columns(tab, cols):
    groups = tab.shape[1]
    col = iota((1, cols), 1)
    chip, tok, grp, slot = col // 8, (col // 4) % 2, (col // 2) % 2, col % 2
    pick = (iota((groups, cols), 0) == chip * 2 + grp).astype(f32)
    every = lax.dot_general(tab, pick, NN, preferred_element_type=f32, precision=lax.Precision.HIGHEST)
    keep = iota((4, cols), 0) == tok * 2 + slot
    return jnp.sum(jnp.where(keep, every, 0.0), axis=0, keepdims=True), tok, slot


def lookup_body(step_ref, table_hbm, last_hbm, ids_hbm, out_ref, table_ref, last_ref, ids_ref, sems):
    copies = [
        pltpu.make_async_copy(source, target, sems.at[k])
        for k, (source, target) in enumerate(((ids_hbm, ids_ref), (last_hbm, last_ref), (table_hbm, table_ref)))
    ]
    for copy in copies:
        copy.start()
    toks, rows, width = table_ref.shape
    cols = out_ref.shape[0]
    copies[0].wait()
    ids, tok, _ = slot_columns(ids_ref[...].astype(f32), cols)
    ids = ids + tok.astype(f32) * rows
    column = jnp.transpose(jnp.broadcast_to(ids, (8, cols)))[:, 0:1]
    copies[1].wait()
    weights = []
    for j in range(toks):
        elapsed = (step_ref[0] - last_ref[j : j + 1, :]).astype(f32)
        factor = jnp.exp(elapsed * decay_log)
        hit = iota((cols, rows), 1).astype(f32) + (j * rows) == column
        weights.append(jnp.where(hit, factor, 0.0))
    copies[2].wait()
    total = jnp.zeros((cols, width), f32)
    for j in range(toks):
        total = total + lax.dot_general(
            weights[j], table_ref[j], NN, preferred_element_type=f32, precision=lax.Precision.HIGHEST
        )
    out_ref[...] = total


def list_targets(slots, half):
    group = (iota(slots.shape, 1) >= half).astype(i32)
    return (slots // 2) * 4 + group * 2 + slots % 2


def place_body(target_ref, place_ref):
    _, lines, width = place_ref.shape
    for k in range(2):
        place_ref[k] = (iota((lines, width), 1) == target_ref[:, k : k + 1]).astype(bf16)


def own_target(targets, token):
    return jnp.sum(jnp.where(iota(targets.shape, 0) == token, targets, 0), axis=0, keepdims=True)


def forward_body(
    where_ref, own_ref, heads_ref, slots_ref, head_ref, order_ref, z_ref, xp_ref, xm_ref, xa_ref, xb_ref,
    normed_in_ref, inv_in_ref, active_ref, slope_ref, normed_out_ref, inv_out_ref, logit_ref, up_ref, down_ref,
    target_ref, all_ref, total_ref, input_ref, choice_ref,
):
    start = 0
    for ref in (z_ref, xp_ref, xm_ref, xa_ref, xb_ref):
        all_ref[start : start + ref.shape[0]] = ref[...]
        start += ref.shape[0]
    width, lists = own_ref.shape
    samples = slots_ref.shape[1]
    toks = slots_ref.shape[0] // 2
    head = width // toks
    rows, hidden = all_ref.shape
    for k in range(2):
        choice_ref[k * width : (k + 1) * width] = (iota((width, rows), 0) == order_ref[k : k + 1, :]).astype(bf16)
    targets = list_targets(slots_ref[0:toks, :], samples // 2)
    target_ref[...] = targets
    row = iota((lists, samples), 0)
    mixed = []
    for t in range(toks):
        one = (row == targets[t : t + 1, :]).astype(bf16)
        mixed.append(dot2(heads_ref[t * head : (t + 1) * head, :], one))
    one_own = (row == own_target(targets, where_ref[0])).astype(bf16)
    value = dot2(own_ref[...], one_own) + jnp.concatenate(mixed, axis=0)
    centre = jnp.mean(value, axis=0, keepdims=True)
    shifted = value - centre
    inverse = lax.rsqrt(jnp.mean(shifted * shifted, axis=0, keepdims=True) + norm_eps)
    normed = shifted * inverse
    normed_in_ref[...] = normed
    inv_in_ref[...] = inverse
    input_ref[...] = jnp.transpose(normed.astype(bf16))
    total_ref[...] = normed
    chunk = 256

    @pl.loop(0, hidden // chunk)
    def _(i):
        cols = pl.ds(pl.multiple_of(i * chunk, chunk), chunk)
        both = dot(choice_ref[...], all_ref[:, cols]).astype(bf16)
        up, down = both[:width], both[width:]
        up_ref[:, cols] = up
        down_ref[:, cols] = down
        pre = dot(input_ref[...], up)
        cumulative = 0.5 * (1.0 + lax.erf(pre * (1.0 / math.sqrt(2.0))))
        density = jnp.exp(-0.5 * pre * pre) * (1.0 / math.sqrt(2.0 * math.pi))
        active = (pre * cumulative).astype(bf16)
        active_ref[:, cols] = active
        slope_ref[:, cols] = cumulative + pre * density
        total_ref[...] += dot(down, active, NT)

    value = total_ref[...]
    centre = jnp.mean(value, axis=0, keepdims=True)
    shifted = value - centre
    inverse = lax.rsqrt(jnp.mean(shifted * shifted, axis=0, keepdims=True) + norm_eps)
    normed = shifted * inverse
    normed_out_ref[...] = normed
    inv_out_ref[...] = inverse
    logit_ref[...] = jnp.sum(normed * head_ref[...], axis=0, keepdims=True)


def norm_back(grad_in, normed, inverse):
    first = jnp.mean(grad_in, axis=0, keepdims=True)
    second = jnp.mean(grad_in * normed, axis=0, keepdims=True)
    return inverse * (grad_in - first - normed * second)


def grad_down_body(
    place_ref, logit_ref, label_ref, head_ref, normed_out_ref, inv_out_ref, active_ref,
    grad_sum_ref, grad_out_ref, kept_ref, next_ref, far_ref, last_ref, padded_ref,
):
    dlogit = jax.nn.sigmoid(logit_ref[...]) - label_ref[...]
    grad = norm_back(dlogit * head_ref[...], normed_out_ref[...], inv_out_ref[...])
    grad_sum_ref[...] = grad
    rounded = grad.astype(bf16)
    grad_out_ref[...] = jnp.transpose(rounded)
    lines, half = kept_ref.shape
    for k in range(2):
        padded_ref[k] = dot(place_ref[k], rounded).astype(bf16)
    chunk = 256

    @pl.loop(0, half // chunk)
    def _(i):
        cols = pl.ds(pl.multiple_of(i * chunk, chunk), chunk)
        more = pl.ds(pl.multiple_of(half + i * chunk, chunk), chunk)
        value = dot(padded_ref[0], active_ref[:, cols]) + dot(padded_ref[1], active_ref[:, more])
        kept_ref[:, cols] = value[0:lines]
        next_ref[:, cols] = value[lines : 2 * lines].astype(bf16)
        far_ref[:, cols] = value[2 * lines : 3 * lines].astype(bf16)
        last_ref[:, cols] = value[3 * lines :].astype(bf16)


def grad_rows_body(
    where_ref, target_ref, grad_sum_ref, grad_out_ref, slope_ref, up_ref, down_ref, normed_in_ref, inv_in_ref,
    own_ref, back_ref, total_ref,
):
    lists, width = own_ref.shape
    toks, samples = target_ref.shape
    head = width // toks
    total_ref[...] = grad_sum_ref[...]
    chunk = 256

    @pl.loop(0, slope_ref.shape[1] // chunk)
    def _(i):
        cols = pl.ds(pl.multiple_of(i * chunk, chunk), chunk)
        grad = dot(grad_out_ref[...], down_ref[:, cols])
        grad_pre = (grad * slope_ref[:, cols]).astype(bf16)
        total_ref[...] += dot(up_ref[:, cols], grad_pre, NT)

    mixed = norm_back(total_ref[...], normed_in_ref[...], inv_in_ref[...])
    targets = target_ref[...]
    row = iota((lists, samples), 0)
    one_own = (row == own_target(targets, where_ref[0])).astype(bf16)
    hi, lo = split(mixed)
    own_ref[...] = dot(one_own, hi, NT) + dot(one_own, lo, NT)
    for t in range(toks):
        one = (row == targets[t : t + 1, :]).astype(bf16)
        span = slice(t * head, (t + 1) * head)
        back_ref[span, :] = (dot(hi[span], one, NT) + dot(lo[span], one, NT)).astype(bf16)


def list_body(own_ref, returned_ref, out_ref):
    returned = jnp.transpose(returned_ref[...].astype(f32))
    out_ref[...] = (own_ref[...] + returned).astype(bf16).reshape(out_ref.shape)


def update_body(
    step_ref, table_ref, accum_ref, last_ref, ids_ref, counts_ref, back_ref,
    table_out_ref, accum_out_ref,
):
    toks, rows, width = table_ref.shape
    cols = back_ref.shape[0] * back_ref.shape[1]
    ids, tok, slot = slot_columns(ids_ref[...].astype(f32), cols)
    counts = counts_ref[...].astype(f32)
    four = jnp.concatenate([counts[0:1], counts[0:1], counts[1:2], counts[1:2]], axis=0)
    have, _, _ = slot_columns(four, cols)
    valid = slot.astype(f32) < have
    row = iota((rows, cols), 0).astype(f32)
    back = back_ref[...].astype(f32).reshape(cols, width).astype(bf16)
    for j in range(toks):
        named = jnp.where((tok == j) & valid, ids, -1.0)
        hit = (row == named).astype(f32)
        grads = dot(hit.astype(bf16), back)
        square = grads * grads
        touched = jnp.max(hit, axis=1, keepdims=True) > 0.0
        flat = jnp.concatenate(
            [last_ref[j : j + 1, :].astype(f32), accum_ref[j : j + 1, :], jnp.zeros((6, rows), f32)], axis=0
        )
        upright = jnp.transpose(flat)
        factor = jnp.exp((step_ref[0].astype(f32) - upright[:, 0:1]) * decay_log)
        accum = upright[:, 1:2] + jnp.mean(square, axis=1, keepdims=True)
        wide = jnp.transpose(jnp.broadcast_to(accum, (rows, 8)))
        accum_out_ref[j : j + 1, :] = wide[0:1, :]
        table = table_ref[j]
        updated = table * factor - learn_rate * grads * lax.rsqrt(accum)
        table_out_ref[j] = jnp.where(touched, updated, table)


def ring(value, axis, size, shift):
    return lax.ppermute(value, axis, [(i, (i + shift) % size) for i in range(size)])


def flip(value, axis, size, bit):
    return lax.ppermute(value, axis, [(i, i ^ bit) for i in range(size)])


def weight_order(x, z, core, n_x, n_z, steps_z, part):
    block = part // n_z
    third = block // 4
    line = np.arange(4 * part)
    step_x = np.array([0, -1, 1, 2])[line // part]
    step_z = np.asarray(steps_z)[(line % part) // block]
    inner = line % block
    other = inner // (2 * third)
    is_down = (inner // third) % 2
    r = inner % third
    chip = ((x + step_x + n_x) % n_x) * n_z + (z + step_z + n_z) % n_z
    owner = jnp.where(core == 0, other, 1 - other)
    target = (chip * 2 + owner) * third + r
    return jnp.stack([jnp.where(is_down == 0, target, -1), jnp.where(is_down == 1, target, -1)]).astype(i32)


def place_order(x, z, n_x, n_z, third):
    block = 4 * third
    line = np.arange(n_x * n_z * block)
    step_x, pos, inner = line // (n_z * block), line // block % n_z, line % block
    chip = (x + step_x) % n_x * n_z + (z ^ (pos // 2 + pos % 2 * (n_z // 2)))
    row = chip * 2 * third + inner % (2 * third)
    second = inner // (2 * third)
    return jnp.stack([jnp.where(second == 0, row, -1), jnp.where(second == 1, row, -1)], axis=1).astype(i32)


def on_device(
    row_table, row_accum, last_step, step_now, row_ids, row_counts, sample_slots, labels, up_weight, down_weight, out_weight
):
    n_tok, n_x, n_z = lax.axis_size("tok"), lax.axis_size("x"), lax.axis_size("z")
    _, _, width = row_table.shape
    toks, batch = sample_slots.shape
    groups, capacity = row_ids.shape[2:]
    head = width // toks
    hidden = up_weight.shape[2]
    lists = 2 * groups * capacity
    samples = 2 * batch
    core = lax.axis_index("core")
    token = lax.axis_index("tok") * 2 + core

    ids = row_ids[:, 0].transpose(0, 2, 1).reshape(2 * capacity, groups)
    looked = call(
        lookup_body,
        sds((lists, width)),
        "lookup",
        scratch=(
            pltpu.VMEM(row_table.shape, f32), pltpu.VMEM(last_step.shape, i32), pltpu.VMEM(ids.shape, i32),
            pltpu.SemaphoreType.DMA((3,)),
        ),
        n_in=4, smem=1, flops=10**9, nbytes=2 * 10**6, away=3, room=48,
    )(step_now, row_table, last_step, ids)
    sent = looked.astype(f16).reshape(groups, 2 * capacity, width)
    got = lax.all_to_all(sent, ("x", "z", "core"), 0, 0, tiled=True)
    own = got.reshape(lists, width).T
    heads = lax.all_to_all(own.reshape(toks, head, lists), ("tok", "core"), 0, 0, tiled=True)
    heads = heads.reshape(width, lists).astype(f32)
    own = own.astype(f32)

    both = jnp.concatenate([up_weight, down_weight], axis=0)
    keep = jnp.where(core == 0, both[:, 0], both[:, 1])
    give = jnp.where(core == 0, both[:, 1], both[:, 0])
    piece = jnp.concatenate([keep, flip(give, "core", 2, 1)], axis=0)

    mine = jnp.concatenate([sample_slots, labels[None], jnp.zeros((toks - 1, batch), i32)], axis=0)
    theirs = flip(mine, "core", 2, 1)
    slots = jnp.where(core == 0, jnp.concatenate([mine, theirs], axis=1), jnp.concatenate([theirs, mine], axis=1))
    label_row = slots[toks : toks + 1].astype(f32)
    before, after = ring(piece, "z", n_z, 1), ring(piece, "z", n_z, -1)
    pair = jnp.concatenate([before, piece], axis=0)
    three = jnp.concatenate([before, piece, after], axis=0)
    far_before, far_after = ring(three, "z", n_z, 3), ring(pair, "z", n_z, -3)
    line = jnp.concatenate([three, far_before, far_after], axis=0)
    steps_z = (-1, 0, 1, -4, -3, -2, 2, 3)
    part = line.shape[0]
    x_before, x_after = ring(line, "x", n_x, 1), ring(line, "x", n_x, -1)
    far_a = ring(x_before[: part // 2], "x", n_x, 1)
    far_b = ring(x_after[part // 2 :], "x", n_x, -1)
    order = weight_order(lax.axis_index("x"), lax.axis_index("z"), core, n_x, n_z, steps_z, part)
    third = width // (n_x * n_z * 2)
    lines = n_z * 4 * third
    target = place_order(lax.axis_index("x"), lax.axis_index("z"), n_x, n_z, third)
    place = call(place_body, sds((2, n_x * lines, width), bf16), "place", n_in=1, flops=10**6, nbytes=10**6)(target)

    where = token.reshape(1).astype(i32)
    head_weight = jnp.where(core == 0, out_weight[0], out_weight[1])[:, None]
    full = (samples, hidden)
    weight = sds((width, hidden), bf16)
    normed_in, inv_in, active, slope, normed_out, inv_out, partial, up, down, targets = call(
        forward_body,
        (
            sds((width, samples)), sds((1, samples)), sds(full, bf16), sds(full),
            sds((width, samples)), sds((1, samples)), sds((1, samples)), weight, weight, sds((toks, samples), i32),
        ),
        "forward",
        scratch=(
            pltpu.VMEM((4 * part, hidden), bf16), pltpu.VMEM((width, samples), f32), pltpu.VMEM((samples, width), bf16),
            pltpu.VMEM((2 * width, 4 * part), bf16),
        ),
        n_in=11, smem=1, flops=4 * 10**9, nbytes=10**7, room=24,
    )(where, own, heads, slots, head_weight, order, line, x_before, x_after, far_a, far_b)
    logits = partial + flip(partial, "core", 2, 1)
    there = [flip(logits, "tok", n_tok, k) for k in (1, 2, 3)]
    logits = (logits + there[0]) + (there[1] + there[2])

    block = (lines, hidden // 2)
    grad_sum, grad_out, kept, *away = call(
        grad_down_body,
        (sds((width, samples)), sds((samples, width), bf16), sds(block), sds(block, bf16), sds(block, bf16), sds(block, bf16)),
        "grad_down",
        scratch=(pltpu.VMEM((2, n_x * lines, samples), bf16),),
        n_in=7, flops=2 * 10**9, nbytes=5 * 10**6,
    )(place, logits, label_row, head_weight, normed_out, inv_out, active)
    come = [ring(v, "x", n_x, k + 1) for k, v in enumerate(away)]
    pair = 8 * third
    total = kept + sum(v.astype(f32) for v in come)
    total = [total[k * pair : (k + 1) * pair] for k in range(n_z // 2)]
    total[1:] = [flip(v, "z", n_z, k + 1) for k, v in enumerate(total[1:])]
    total = (total[0] + total[1]) + (total[2] + total[3])
    stay, leave = total[: pair // 2], total[pair // 2 :]
    summed = stay + flip(leave, "z", n_z, n_z // 2)

    own_grads, head_grads = call(
        grad_rows_body,
        (sds((lists, width)), sds((width, lists), bf16)),
        "grad_rows",
        scratch=(pltpu.VMEM((width, samples), f32),),
        n_in=9, smem=1, flops=2 * 10**9, nbytes=8 * 10**6,
    )(where, targets, grad_sum, grad_out, slope, up, down, normed_in, inv_in)
    returned = lax.all_to_all(head_grads.reshape(toks, head, lists), ("tok", "core"), 0, 0, tiled=True)
    list_grads = call(
        list_body, sds((groups, 2 * capacity, width), bf16), "lists", n_in=2, flops=10**6, nbytes=10**6
    )(own_grads, returned.reshape(width, lists))
    back = lax.all_to_all(list_grads, ("x", "z", "core"), 0, 0, tiled=True)
    new_table, new_accum = call(
        update_body,
        (sds(row_table.shape), sds(row_accum.shape)),
        "update",
        n_in=7, smem=1, flops=10**9, nbytes=3 * 10**6,
    )(step_now, row_table, row_accum, last_step, ids, row_counts[:, 0], back)

    summed = jnp.concatenate([summed[: 2 * third], summed[2 * third :]], axis=1)
    low, high = summed[:third], summed[third:]
    stay, leave = jnp.where(core == 0, low, high), jnp.where(core == 0, high, low)
    come = flip(leave, "core", 2, 1)
    grad_down = jnp.where(core == 0, jnp.stack([stay, come], axis=1), jnp.stack([come, stay], axis=1))
    logits = jnp.where(core == 0, logits[0, :batch], logits[0, batch:])
    return (new_table, new_accum, grad_down, logits)


def solution(mesh):
    devices = mesh.devices.reshape(4, 4, 8, 2)
    wide = Mesh(devices, ("tok", "x", "z", "core"))
    smp = ("x", "z", "core")
    return jax.shard_map(
        on_device,
        mesh=wide,
        in_specs=(
            P("tok", smp, None),
            P("tok", smp),
            P("tok", smp),
            P(),
            P("tok", smp, None, None),
            P("tok", smp, None),
            P(None, smp),
            P(smp),
            P(smp, "tok", None),
            P(smp, "tok", None),
            P("tok", None),
        ),
        out_specs=(P("tok", smp, None), P("tok", smp), P(smp, "tok", None), P(smp)),
        check_vma=False,
    )
```

```python
import math

import jax
import jax.numpy as jnp
import numpy as np
from jax import lax
from jax.experimental import pallas as pl
from jax.experimental.pallas import tpu as pltpu
from jax.sharding import Mesh
from jax.sharding import PartitionSpec as P


decay_log = math.log(0.98)
learn_rate = 0.2
norm_eps = 1e-05
f32 = jnp.float32
bf16 = jnp.bfloat16
f16 = jnp.float16
i32 = jnp.int32


NN = (((1,), (0,)), ((), ()))
NT = (((1,), (1,)), ((), ()))
VM = pl.BlockSpec(memory_space=pltpu.VMEM)
SM = pl.BlockSpec(memory_space=pltpu.SMEM)
ANY = pl.BlockSpec(memory_space=pl.ANY)
HBM = pl.BlockSpec(memory_space=pltpu.HBM)


def dot(a, b, dims=NN):
    return lax.dot_general(a, b, dims, preferred_element_type=f32)


def split(v):
    hi = v.astype(bf16)
    return hi, (v - hi.astype(f32)).astype(bf16)


def dot2(v, b, dims=NN):
    hi, lo = split(v)
    return dot(hi, b, dims) + dot(lo, b, dims)


def iota(shape, dim):
    return lax.broadcasted_iota(i32, shape, dim)


def call(body, outs, name, scratch=(), n_in=0, smem=0, flops=0, nbytes=0, room=8, away=0):
    return pl.pallas_call(
        body,
        out_shape=outs,
        in_specs=[SM] * smem + [HBM if name == "lookup" else ANY] * away + [VM] * (n_in - smem - away),
        out_specs=jax.tree.map(lambda _: VM, outs),
        scratch_shapes=list(scratch),
        compiler_params=pltpu.CompilerParams(vmem_limit_bytes=room * 2**20),
        cost_estimate=pl.CostEstimate(flops=flops, bytes_accessed=nbytes, transcendentals=0),
    )


def sds(shape, dtype=f32):
    return jax.ShapeDtypeStruct(shape, dtype)


def slot_columns(tab, cols):
    groups = tab.shape[1]
    col = iota((1, cols), 1)
    chip, tok, grp, slot = col // 8, (col // 4) % 2, (col // 2) % 2, col % 2
    pick = (iota((groups, cols), 0) == chip * 2 + grp).astype(f32)
    every = lax.dot_general(tab, pick, NN, preferred_element_type=f32, precision=lax.Precision.HIGHEST)
    keep = iota((4, cols), 0) == tok * 2 + slot
    return jnp.sum(jnp.where(keep, every, 0.0), axis=0, keepdims=True), tok, slot


def lookup_body(step_ref, table_hbm, last_hbm, ids_hbm, out_ref, table_ref, last_ref, ids_ref, sems):
    copies = [
        pltpu.make_async_copy(source, target, sems.at[k])
        for k, (source, target) in enumerate(((ids_hbm, ids_ref), (last_hbm, last_ref), (table_hbm, table_ref)))
    ]
    for copy in copies:
        copy.start()
    toks, rows, width = table_ref.shape
    cols = out_ref.shape[0]
    copies[0].wait()
    ids, tok, _ = slot_columns(ids_ref[...].astype(f32), cols)
    ids = ids + tok.astype(f32) * rows
    column = jnp.transpose(jnp.broadcast_to(ids, (8, cols)))[:, 0:1]
    copies[1].wait()
    weights = []
    for j in range(toks):
        elapsed = (step_ref[0] - last_ref[j : j + 1, :]).astype(f32)
        factor = jnp.exp(elapsed * decay_log)
        hit = iota((cols, rows), 1).astype(f32) + (j * rows) == column
        weights.append(jnp.where(hit, factor, 0.0))
    copies[2].wait()
    total = jnp.zeros((cols, width), f32)
    for j in range(toks):
        total = total + lax.dot_general(
            weights[j], table_ref[j], NN, preferred_element_type=f32, precision=lax.Precision.HIGHEST
        )
    out_ref[...] = total


def list_targets(slots, half):
    group = (iota(slots.shape, 1) >= half).astype(i32)
    return (slots // 2) * 4 + group * 2 + slots % 2


def place_body(target_ref, place_ref):
    _, lines, width = place_ref.shape
    for k in range(2):
        place_ref[k] = (iota((lines, width), 1) == target_ref[:, k : k + 1]).astype(bf16)


def own_target(targets, token):
    return jnp.sum(jnp.where(iota(targets.shape, 0) == token, targets, 0), axis=0, keepdims=True)


def forward_body(
    where_ref, own_ref, heads_ref, slots_ref, head_ref, order_ref, z_ref, xp_ref, xm_ref, xa_ref, xb_ref,
    normed_in_ref, inv_in_ref, active_ref, slope_ref, normed_out_ref, inv_out_ref, logit_ref, up_ref, down_ref,
    target_ref, all_ref, total_ref, input_ref,
):
    start = 0
    for ref in (z_ref, xp_ref, xm_ref, xa_ref, xb_ref):
        all_ref[start : start + ref.shape[0]] = ref[...]
        start += ref.shape[0]
    width, lists = own_ref.shape
    samples = slots_ref.shape[1]
    toks = slots_ref.shape[0] // 2
    head = width // toks
    rows, hidden = all_ref.shape
    order_up = (iota((width, rows), 0) == order_ref[0:1, :]).astype(bf16)
    order_down = (iota((width, rows), 0) == order_ref[1:2, :]).astype(bf16)
    targets = list_targets(slots_ref[0:toks, :], samples // 2)
    target_ref[...] = targets
    row = iota((lists, samples), 0)
    mixed = []
    for t in range(toks):
        one = (row == targets[t : t + 1, :]).astype(bf16)
        mixed.append(dot2(heads_ref[t * head : (t + 1) * head, :], one))
    one_own = (row == own_target(targets, where_ref[0])).astype(bf16)
    value = dot2(own_ref[...], one_own) + jnp.concatenate(mixed, axis=0)
    centre = jnp.mean(value, axis=0, keepdims=True)
    shifted = value - centre
    inverse = lax.rsqrt(jnp.mean(shifted * shifted, axis=0, keepdims=True) + norm_eps)
    normed = shifted * inverse
    normed_in_ref[...] = normed
    inv_in_ref[...] = inverse
    input_ref[...] = jnp.transpose(normed.astype(bf16))
    total_ref[...] = normed
    chunk = 256

    @pl.loop(0, hidden // chunk)
    def _(i):
        cols = pl.ds(pl.multiple_of(i * chunk, chunk), chunk)
        block = all_ref[:, cols]
        up = dot(order_up, block).astype(bf16)
        down = dot(order_down, block).astype(bf16)
        up_ref[:, cols] = up
        down_ref[:, cols] = down
        pre = dot(input_ref[...], up)
        cumulative = 0.5 * (1.0 + lax.erf(pre * (1.0 / math.sqrt(2.0))))
        density = jnp.exp(-0.5 * pre * pre) * (1.0 / math.sqrt(2.0 * math.pi))
        active = (pre * cumulative).astype(bf16)
        active_ref[:, cols] = active
        slope_ref[:, cols] = cumulative + pre * density
        total_ref[...] += dot(down, active, NT)

    value = total_ref[...]
    centre = jnp.mean(value, axis=0, keepdims=True)
    shifted = value - centre
    inverse = lax.rsqrt(jnp.mean(shifted * shifted, axis=0, keepdims=True) + norm_eps)
    normed = shifted * inverse
    normed_out_ref[...] = normed
    inv_out_ref[...] = inverse
    logit_ref[...] = jnp.sum(normed * head_ref[...], axis=0, keepdims=True)


def norm_back(grad_in, normed, inverse):
    first = jnp.mean(grad_in, axis=0, keepdims=True)
    second = jnp.mean(grad_in * normed, axis=0, keepdims=True)
    return inverse * (grad_in - first - normed * second)


def grad_down_body(
    place_ref, logit_ref, slots_ref, head_ref, normed_out_ref, inv_out_ref, active_ref,
    grad_sum_ref, grad_out_ref, kept_ref, next_ref, far_ref, last_ref, padded_ref,
):
    toks = slots_ref.shape[0] // 2
    labels = slots_ref[toks : toks + 1, :].astype(f32)
    dlogit = jax.nn.sigmoid(logit_ref[...]) - labels
    grad = norm_back(dlogit * head_ref[...], normed_out_ref[...], inv_out_ref[...])
    grad_sum_ref[...] = grad
    rounded = grad.astype(bf16)
    grad_out_ref[...] = jnp.transpose(rounded)
    lines, half = kept_ref.shape
    for k in range(2):
        padded_ref[k] = dot(place_ref[k], rounded).astype(bf16)
    chunk = 256

    @pl.loop(0, half // chunk)
    def _(i):
        cols = pl.ds(pl.multiple_of(i * chunk, chunk), chunk)
        more = pl.ds(pl.multiple_of(half + i * chunk, chunk), chunk)
        value = dot(padded_ref[0], active_ref[:, cols]) + dot(padded_ref[1], active_ref[:, more])
        kept_ref[:, cols] = value[0:lines]
        next_ref[:, cols] = value[lines : 2 * lines].astype(bf16)
        far_ref[:, cols] = value[2 * lines : 3 * lines].astype(bf16)
        last_ref[:, cols] = value[3 * lines :].astype(bf16)


def grad_rows_body(
    where_ref, target_ref, grad_sum_ref, grad_out_ref, slope_ref, up_ref, down_ref, normed_in_ref, inv_in_ref,
    own_ref, back_ref, total_ref,
):
    lists, width = own_ref.shape
    toks, samples = target_ref.shape
    head = width // toks
    total_ref[...] = grad_sum_ref[...]
    chunk = 256

    @pl.loop(0, slope_ref.shape[1] // chunk)
    def _(i):
        cols = pl.ds(pl.multiple_of(i * chunk, chunk), chunk)
        grad = dot(grad_out_ref[...], down_ref[:, cols])
        grad_pre = (grad * slope_ref[:, cols]).astype(bf16)
        total_ref[...] += dot(up_ref[:, cols], grad_pre, NT)

    mixed = norm_back(total_ref[...], normed_in_ref[...], inv_in_ref[...])
    targets = target_ref[...]
    row = iota((lists, samples), 0)
    one_own = (row == own_target(targets, where_ref[0])).astype(bf16)
    hi, lo = split(mixed)
    own_ref[...] = dot(one_own, hi, NT) + dot(one_own, lo, NT)
    for t in range(toks):
        one = (row == targets[t : t + 1, :]).astype(bf16)
        span = slice(t * head, (t + 1) * head)
        back_ref[span, :] = (dot(hi[span], one, NT) + dot(lo[span], one, NT)).astype(bf16)


def list_body(own_ref, returned_ref, out_ref):
    returned = jnp.transpose(returned_ref[...].astype(f32))
    out_ref[...] = (own_ref[...] + returned).astype(bf16).reshape(out_ref.shape)


def update_body(
    step_ref, table_ref, accum_ref, last_ref, ids_ref, counts_ref, back_ref,
    table_out_ref, accum_out_ref,
):
    toks, rows, width = table_ref.shape
    cols = back_ref.shape[0] * back_ref.shape[1]
    ids, tok, slot = slot_columns(ids_ref[...].astype(f32), cols)
    counts = counts_ref[...].astype(f32)
    four = jnp.concatenate([counts[0:1], counts[0:1], counts[1:2], counts[1:2]], axis=0)
    have, _, _ = slot_columns(four, cols)
    valid = slot.astype(f32) < have
    row = iota((rows, cols), 0).astype(f32)
    back = back_ref[...].astype(f32).reshape(cols, width).astype(bf16)
    for j in range(toks):
        named = jnp.where((tok == j) & valid, ids, -1.0)
        hit = (row == named).astype(f32)
        grads = dot(hit.astype(bf16), back)
        square = grads * grads
        touched = jnp.max(hit, axis=1, keepdims=True) > 0.0
        flat = jnp.concatenate(
            [last_ref[j : j + 1, :].astype(f32), accum_ref[j : j + 1, :], jnp.zeros((6, rows), f32)], axis=0
        )
        upright = jnp.transpose(flat)
        factor = jnp.exp((step_ref[0].astype(f32) - upright[:, 0:1]) * decay_log)
        accum = upright[:, 1:2] + jnp.mean(square, axis=1, keepdims=True)
        wide = jnp.transpose(jnp.broadcast_to(accum, (rows, 8)))
        accum_out_ref[j : j + 1, :] = wide[0:1, :]
        table = table_ref[j]
        updated = table * factor - learn_rate * grads * lax.rsqrt(accum)
        table_out_ref[j] = jnp.where(touched, updated, table)


def ring(value, axis, size, shift):
    return lax.ppermute(value, axis, [(i, (i + shift) % size) for i in range(size)])


def flip(value, axis, size, bit):
    return lax.ppermute(value, axis, [(i, i ^ bit) for i in range(size)])


def weight_order(x, z, core, n_x, n_z, steps_z, part):
    block = part // n_z
    third = block // 4
    line = np.arange(4 * part)
    step_x = np.array([0, -1, 1, 2])[line // part]
    step_z = np.asarray(steps_z)[(line % part) // block]
    inner = line % block
    other = inner // (2 * third)
    is_down = (inner // third) % 2
    r = inner % third
    chip = ((x + step_x + n_x) % n_x) * n_z + (z + step_z + n_z) % n_z
    owner = jnp.where(core == 0, other, 1 - other)
    target = (chip * 2 + owner) * third + r
    return jnp.stack([jnp.where(is_down == 0, target, -1), jnp.where(is_down == 1, target, -1)]).astype(i32)


def place_order(x, z, n_x, n_z, third):
    block = 4 * third
    line = np.arange(n_x * n_z * block)
    step_x, pos, inner = line // (n_z * block), line // block % n_z, line % block
    chip = (x + step_x) % n_x * n_z + (z ^ (pos // 2 + pos % 2 * (n_z // 2)))
    row = chip * 2 * third + inner % (2 * third)
    second = inner // (2 * third)
    return jnp.stack([jnp.where(second == 0, row, -1), jnp.where(second == 1, row, -1)], axis=1).astype(i32)


def on_device(
    row_table, row_accum, last_step, step_now, row_ids, row_counts, sample_slots, labels, up_weight, down_weight, out_weight
):
    n_tok, n_x, n_z = lax.axis_size("tok"), lax.axis_size("x"), lax.axis_size("z")
    _, _, width = row_table.shape
    toks, batch = sample_slots.shape
    groups, capacity = row_ids.shape[2:]
    head = width // toks
    hidden = up_weight.shape[2]
    lists = 2 * groups * capacity
    samples = 2 * batch
    core = lax.axis_index("core")
    token = lax.axis_index("tok") * 2 + core

    ids = row_ids[:, 0].transpose(0, 2, 1).reshape(2 * capacity, groups)
    looked = call(
        lookup_body,
        sds((lists, width)),
        "lookup",
        scratch=(
            pltpu.VMEM(row_table.shape, f32), pltpu.VMEM(last_step.shape, i32), pltpu.VMEM(ids.shape, i32),
            pltpu.SemaphoreType.DMA((3,)),
        ),
        n_in=4, smem=1, flops=10**9, nbytes=2 * 10**6, away=3, room=48,
    )(step_now, row_table, last_step, ids)
    sent = looked.astype(f16).reshape(groups, 2 * capacity, width)
    got = lax.all_to_all(sent, ("x", "z", "core"), 0, 0, tiled=True)
    own = got.reshape(lists, width).T
    heads = lax.all_to_all(own.reshape(toks, head, lists), ("tok", "core"), 0, 0, tiled=True)
    heads = heads.reshape(width, lists).astype(f32)
    own = own.astype(f32)

    both = jnp.concatenate([up_weight, down_weight], axis=0)
    keep = jnp.where(core == 0, both[:, 0], both[:, 1])
    give = jnp.where(core == 0, both[:, 1], both[:, 0])
    piece = jnp.concatenate([keep, flip(give, "core", 2, 1)], axis=0)

    mine = jnp.concatenate([sample_slots, labels[None], jnp.zeros((toks - 1, batch), i32)], axis=0)
    theirs = flip(mine, "core", 2, 1)
    slots = jnp.where(core == 0, jnp.concatenate([mine, theirs], axis=1), jnp.concatenate([theirs, mine], axis=1))
    before, after = ring(piece, "z", n_z, 1), ring(piece, "z", n_z, -1)
    pair = jnp.concatenate([before, piece], axis=0)
    three = jnp.concatenate([before, piece, after], axis=0)
    far_before, far_after = ring(three, "z", n_z, 3), ring(pair, "z", n_z, -3)
    line = jnp.concatenate([three, far_before, far_after], axis=0)
    steps_z = (-1, 0, 1, -4, -3, -2, 2, 3)
    part = line.shape[0]
    x_before, x_after = ring(line, "x", n_x, 1), ring(line, "x", n_x, -1)
    far_a = ring(x_before[: part // 2], "x", n_x, 1)
    far_b = ring(x_after[part // 2 :], "x", n_x, -1)
    order = weight_order(lax.axis_index("x"), lax.axis_index("z"), core, n_x, n_z, steps_z, part)
    third = width // (n_x * n_z * 2)
    lines = n_z * 4 * third
    target = place_order(lax.axis_index("x"), lax.axis_index("z"), n_x, n_z, third)
    place = call(place_body, sds((2, n_x * lines, width), bf16), "place", n_in=1, flops=10**6, nbytes=10**6)(target)

    where = token.reshape(1).astype(i32)
    head_weight = jnp.where(core == 0, out_weight[0], out_weight[1])[:, None]
    full = (samples, hidden)
    weight = sds((width, hidden), bf16)
    normed_in, inv_in, active, slope, normed_out, inv_out, partial, up, down, targets = call(
        forward_body,
        (
            sds((width, samples)), sds((1, samples)), sds(full, bf16), sds(full),
            sds((width, samples)), sds((1, samples)), sds((1, samples)), weight, weight, sds((toks, samples), i32),
        ),
        "forward",
        scratch=(
            pltpu.VMEM((4 * part, hidden), bf16), pltpu.VMEM((width, samples), f32), pltpu.VMEM((samples, width), bf16),
        ),
        n_in=11, smem=1, flops=4 * 10**9, nbytes=10**7, room=40,
    )(where, own, heads, slots, head_weight, order, line, x_before, x_after, far_a, far_b)
    logits = partial + flip(partial, "core", 2, 1)
    there = [flip(logits, "tok", n_tok, k) for k in (1, 2, 3)]
    logits = (logits + there[0]) + (there[1] + there[2])

    block = (lines, hidden // 2)
    grad_sum, grad_out, kept, *away = call(
        grad_down_body,
        (sds((width, samples)), sds((samples, width), bf16), sds(block), sds(block, bf16), sds(block, bf16), sds(block, bf16)),
        "grad_down",
        scratch=(pltpu.VMEM((2, n_x * lines, samples), bf16),),
        n_in=7, flops=2 * 10**9, nbytes=5 * 10**6,
    )(place, logits, slots, head_weight, normed_out, inv_out, active)
    come = [ring(v, "x", n_x, k + 1) for k, v in enumerate(away)]
    pair = 8 * third
    total = kept + sum(v.astype(f32) for v in come)
    total = [total[k * pair : (k + 1) * pair] for k in range(n_z // 2)]
    total[1:] = [flip(v, "z", n_z, k + 1) for k, v in enumerate(total[1:])]
    total = (total[0] + total[1]) + (total[2] + total[3])
    stay, leave = total[: pair // 2], total[pair // 2 :]
    summed = stay + flip(leave, "z", n_z, n_z // 2)

    own_grads, head_grads = call(
        grad_rows_body,
        (sds((lists, width)), sds((width, lists), bf16)),
        "grad_rows",
        scratch=(pltpu.VMEM((width, samples), f32),),
        n_in=9, smem=1, flops=2 * 10**9, nbytes=8 * 10**6,
    )(where, targets, grad_sum, grad_out, slope, up, down, normed_in, inv_in)
    returned = lax.all_to_all(head_grads.reshape(toks, head, lists), ("tok", "core"), 0, 0, tiled=True)
    list_grads = call(
        list_body, sds((groups, 2 * capacity, width), bf16), "lists", n_in=2, flops=10**6, nbytes=10**6
    )(own_grads, returned.reshape(width, lists))
    back = lax.all_to_all(list_grads, ("x", "z", "core"), 0, 0, tiled=True)
    new_table, new_accum = call(
        update_body,
        (sds(row_table.shape), sds(row_accum.shape)),
        "update",
        n_in=7, smem=1, flops=10**9, nbytes=3 * 10**6,
    )(step_now, row_table, row_accum, last_step, ids, row_counts[:, 0], back)

    summed = jnp.concatenate([summed[: 2 * third], summed[2 * third :]], axis=1)
    low, high = summed[:third], summed[third:]
    stay, leave = jnp.where(core == 0, low, high), jnp.where(core == 0, high, low)
    come = flip(leave, "core", 2, 1)
    grad_down = jnp.where(core == 0, jnp.stack([stay, come], axis=1), jnp.stack([come, stay], axis=1))
    logits = jnp.where(core == 0, logits[0, :batch], logits[0, batch:])
    return (new_table, new_accum, grad_down, logits)


def solution(mesh):
    devices = mesh.devices.reshape(4, 4, 8, 2)
    wide = Mesh(devices, ("tok", "x", "z", "core"))
    smp = ("x", "z", "core")
    return jax.shard_map(
        on_device,
        mesh=wide,
        in_specs=(
            P("tok", smp, None),
            P("tok", smp),
            P("tok", smp),
            P(),
            P("tok", smp, None, None),
            P("tok", smp, None),
            P(None, smp),
            P(smp),
            P(smp, "tok", None),
            P(smp, "tok", None),
            P("tok", None),
        ),
        out_specs=(P("tok", smp, None), P("tok", smp), P(smp, "tok", None), P(smp)),
        check_vma=False,
    )
```

```python
import math

import jax
import jax.numpy as jnp
import numpy as np
from jax import lax
from jax.experimental import pallas as pl
from jax.experimental.pallas import tpu as pltpu
from jax.sharding import Mesh
from jax.sharding import PartitionSpec as P


decay_log = math.log(0.98)
learn_rate = 0.2
norm_eps = 1e-05
f32 = jnp.float32
bf16 = jnp.bfloat16
f16 = jnp.float16
i32 = jnp.int32


NN = (((1,), (0,)), ((), ()))
NT = (((1,), (1,)), ((), ()))
VM = pl.BlockSpec(memory_space=pltpu.VMEM)
SM = pl.BlockSpec(memory_space=pltpu.SMEM)
ANY = pl.BlockSpec(memory_space=pl.ANY)
HBM = pl.BlockSpec(memory_space=pltpu.HBM)


def dot(a, b, dims=NN):
    return lax.dot_general(a, b, dims, preferred_element_type=f32)


def split(v):
    hi = v.astype(bf16)
    return hi, (v - hi.astype(f32)).astype(bf16)


def dot2(v, b, dims=NN):
    hi, lo = split(v)
    return dot(hi, b, dims) + dot(lo, b, dims)


def iota(shape, dim):
    return lax.broadcasted_iota(i32, shape, dim)


def call(body, outs, name, scratch=(), n_in=0, smem=0, flops=0, nbytes=0, room=8, away=0):
    return pl.pallas_call(
        body,
        out_shape=outs,
        in_specs=[SM] * smem + [HBM if name == "lookup" else ANY] * away + [VM] * (n_in - smem - away),
        out_specs=jax.tree.map(lambda _: VM, outs),
        scratch_shapes=list(scratch),
        compiler_params=pltpu.CompilerParams(vmem_limit_bytes=room * 2**20),
        cost_estimate=pl.CostEstimate(flops=flops, bytes_accessed=nbytes, transcendentals=0),
    )


def sds(shape, dtype=f32):
    return jax.ShapeDtypeStruct(shape, dtype)


def slot_columns(tab, cols):
    groups = tab.shape[1]
    col = iota((1, cols), 1)
    chip, tok, grp, slot = col // 8, (col // 4) % 2, (col // 2) % 2, col % 2
    pick = (iota((groups, cols), 0) == chip * 2 + grp).astype(f32)
    every = lax.dot_general(tab, pick, NN, preferred_element_type=f32, precision=lax.Precision.HIGHEST)
    keep = iota((4, cols), 0) == tok * 2 + slot
    return jnp.sum(jnp.where(keep, every, 0.0), axis=0, keepdims=True), tok, slot


def lookup_body(step_ref, table_hbm, last_hbm, ids_hbm, out_ref, table_ref, last_ref, ids_ref, sems):
    copies = [
        pltpu.make_async_copy(source, target, sems.at[k])
        for k, (source, target) in enumerate(((ids_hbm, ids_ref), (last_hbm, last_ref), (table_hbm, table_ref)))
    ]
    for copy in copies:
        copy.start()
    toks, rows, width = table_ref.shape
    cols = out_ref.shape[0] * out_ref.shape[1]
    copies[0].wait()
    ids, tok, _ = slot_columns(ids_ref[...].astype(f32), cols)
    ids = ids + tok.astype(f32) * rows
    column = jnp.transpose(jnp.broadcast_to(ids, (8, cols)))[:, 0:1]
    copies[1].wait()
    weights = []
    for j in range(toks):
        elapsed = (step_ref[0] - last_ref[j : j + 1, :]).astype(f32)
        factor = jnp.exp(elapsed * decay_log)
        hit = iota((cols, rows), 1).astype(f32) + (j * rows) == column
        weights.append(jnp.where(hit, factor, 0.0))
    copies[2].wait()
    total = jnp.zeros((cols, width), f32)
    for j in range(toks):
        total = total + lax.dot_general(
            weights[j], table_ref[j], NN, preferred_element_type=f32, precision=lax.Precision.HIGHEST
        )
    out_ref[...] = total.reshape(out_ref.shape)


def list_targets(slots, half):
    group = (iota(slots.shape, 1) >= half).astype(i32)
    return (slots // 2) * 4 + group * 2 + slots % 2


def place_body(target_ref, place_ref):
    _, lines, width = place_ref.shape
    for k in range(2):
        place_ref[k] = (iota((lines, width), 1) == target_ref[:, k : k + 1]).astype(bf16)


def own_target(targets, token):
    return jnp.sum(jnp.where(iota(targets.shape, 0) == token, targets, 0), axis=0, keepdims=True)


def forward_body(
    where_ref, own_ref, heads_ref, mine_ref, theirs_ref, head_ref, order_ref, z_ref, xp_ref, xm_ref, xa_ref, xb_ref,
    normed_in_ref, inv_in_ref, active_ref, slope_ref, normed_out_ref, inv_out_ref, logit_ref, up_ref, down_ref,
    target_ref, label_ref, all_ref, total_ref, input_ref,
):
    start = 0
    for ref in (z_ref, xp_ref, xm_ref, xa_ref, xb_ref):
        all_ref[start : start + ref.shape[0]] = ref[...]
        start += ref.shape[0]
    width, lists = own_ref.shape
    mine, theirs = mine_ref[...], theirs_ref[...]
    first = where_ref[0] % 2 == 0
    slots = jnp.concatenate([jnp.where(first, mine, theirs), jnp.where(first, theirs, mine)], axis=1)
    samples = slots.shape[1]
    toks = slots.shape[0] // 2
    head = width // toks
    rows, hidden = all_ref.shape
    targets = list_targets(slots[0:toks, :], samples // 2)
    target_ref[...] = targets
    label_ref[...] = slots[toks : toks + 1, :].astype(f32)
    row = iota((lists, samples), 0)
    mixed = []
    for t in range(toks):
        one = (row == targets[t : t + 1, :]).astype(bf16)
        mixed.append(dot2(heads_ref[t * head : (t + 1) * head, :], one))
    one_own = (row == own_target(targets, where_ref[0])).astype(bf16)
    value = dot2(own_ref[...], one_own) + jnp.concatenate(mixed, axis=0)
    centre = jnp.mean(value, axis=0, keepdims=True)
    shifted = value - centre
    inverse = lax.rsqrt(jnp.mean(shifted * shifted, axis=0, keepdims=True) + norm_eps)
    normed = shifted * inverse
    normed_in_ref[...] = normed
    inv_in_ref[...] = inverse
    input_ref[...] = jnp.transpose(normed.astype(bf16))
    total_ref[...] = normed
    order_up = (iota((width, rows), 0) == order_ref[0:1, :]).astype(bf16)
    order_down = (iota((width, rows), 0) == order_ref[1:2, :]).astype(bf16)
    chunk = 256

    @pl.loop(0, hidden // chunk)
    def _(i):
        cols = pl.ds(pl.multiple_of(i * chunk, chunk), chunk)
        block = all_ref[:, cols]
        up = dot(order_up, block).astype(bf16)
        down = dot(order_down, block).astype(bf16)
        up_ref[:, cols] = up
        down_ref[:, cols] = down
        pre = dot(input_ref[...], up)
        cumulative = 0.5 * (1.0 + lax.erf(pre * (1.0 / math.sqrt(2.0))))
        density = jnp.exp(-0.5 * pre * pre) * (1.0 / math.sqrt(2.0 * math.pi))
        active = (pre * cumulative).astype(bf16)
        active_ref[:, cols] = active
        slope_ref[:, cols] = cumulative + pre * density
        total_ref[...] += dot(down, active, NT)

    value = total_ref[...]
    centre = jnp.mean(value, axis=0, keepdims=True)
    shifted = value - centre
    inverse = lax.rsqrt(jnp.mean(shifted * shifted, axis=0, keepdims=True) + norm_eps)
    normed = shifted * inverse
    normed_out_ref[...] = normed
    inv_out_ref[...] = inverse
    logit_ref[...] = jnp.sum(normed * head_ref[...], axis=0, keepdims=True)


def norm_back(grad_in, normed, inverse):
    first = jnp.mean(grad_in, axis=0, keepdims=True)
    second = jnp.mean(grad_in * normed, axis=0, keepdims=True)
    return inverse * (grad_in - first - normed * second)


def grad_down_body(
    place_ref, logit_ref, label_ref, head_ref, normed_out_ref, inv_out_ref, active_ref,
    grad_sum_ref, grad_out_ref, kept_ref, next_ref, far_ref, last_ref, padded_ref,
):
    dlogit = jax.nn.sigmoid(logit_ref[...]) - label_ref[...]
    grad = norm_back(dlogit * head_ref[...], normed_out_ref[...], inv_out_ref[...])
    grad_sum_ref[...] = grad
    rounded = grad.astype(bf16)
    grad_out_ref[...] = jnp.transpose(rounded)
    lines, half = kept_ref.shape
    for k in range(2):
        padded_ref[k] = dot(place_ref[k], rounded).astype(bf16)
    chunk = 256

    @pl.loop(0, half // chunk)
    def _(i):
        cols = pl.ds(pl.multiple_of(i * chunk, chunk), chunk)
        more = pl.ds(pl.multiple_of(half + i * chunk, chunk), chunk)
        value = dot(padded_ref[0], active_ref[:, cols]) + dot(padded_ref[1], active_ref[:, more])
        kept_ref[:, cols] = value[0:lines]
        next_ref[:, cols] = value[lines : 2 * lines].astype(bf16)
        far_ref[:, cols] = value[2 * lines : 3 * lines].astype(bf16)
        last_ref[:, cols] = value[3 * lines :].astype(bf16)


def grad_rows_body(
    where_ref, target_ref, grad_sum_ref, grad_out_ref, slope_ref, up_ref, down_ref, normed_in_ref, inv_in_ref,
    own_ref, back_ref, total_ref,
):
    lists, width = own_ref.shape
    toks, samples = target_ref.shape
    head = width // toks
    total_ref[...] = grad_sum_ref[...]
    chunk = 256

    @pl.loop(0, slope_ref.shape[1] // chunk)
    def _(i):
        cols = pl.ds(pl.multiple_of(i * chunk, chunk), chunk)
        grad = dot(grad_out_ref[...], down_ref[:, cols])
        grad_pre = (grad * slope_ref[:, cols]).astype(bf16)
        total_ref[...] += dot(up_ref[:, cols], grad_pre, NT)

    mixed = norm_back(total_ref[...], normed_in_ref[...], inv_in_ref[...])
    targets = target_ref[...]
    row = iota((lists, samples), 0)
    one_own = (row == own_target(targets, where_ref[0])).astype(bf16)
    hi, lo = split(mixed)
    own_ref[...] = dot(one_own, hi, NT) + dot(one_own, lo, NT)
    for t in range(toks):
        one = (row == targets[t : t + 1, :]).astype(bf16)
        span = slice(t * head, (t + 1) * head)
        back_ref[span, :] = (dot(hi[span], one, NT) + dot(lo[span], one, NT)).astype(bf16)


def list_body(own_ref, returned_ref, out_ref):
    returned = jnp.transpose(returned_ref[...].astype(f32))
    out_ref[...] = (own_ref[...] + returned).astype(bf16).reshape(out_ref.shape)


def update_body(
    step_ref, table_ref, accum_ref, last_ref, ids_ref, counts_ref, back_ref,
    table_out_ref, accum_out_ref,
):
    toks, rows, width = table_ref.shape
    cols = back_ref.shape[0] * back_ref.shape[1]
    ids, tok, slot = slot_columns(ids_ref[...].astype(f32), cols)
    counts = counts_ref[...].astype(f32)
    four = jnp.concatenate([counts[0:1], counts[0:1], counts[1:2], counts[1:2]], axis=0)
    have, _, _ = slot_columns(four, cols)
    valid = slot.astype(f32) < have
    row = iota((rows, cols), 0).astype(f32)
    back = back_ref[...].astype(f32).reshape(cols, width).astype(bf16)
    for j in range(toks):
        named = jnp.where((tok == j) & valid, ids, -1.0)
        hit = (row == named).astype(f32)
        grads = dot(hit.astype(bf16), back)
        square = grads * grads
        touched = jnp.max(hit, axis=1, keepdims=True) > 0.0
        flat = jnp.concatenate(
            [last_ref[j : j + 1, :].astype(f32), accum_ref[j : j + 1, :], jnp.zeros((6, rows), f32)], axis=0
        )
        upright = jnp.transpose(flat)
        factor = jnp.exp((step_ref[0].astype(f32) - upright[:, 0:1]) * decay_log)
        accum = upright[:, 1:2] + jnp.mean(square, axis=1, keepdims=True)
        wide = jnp.transpose(jnp.broadcast_to(accum, (rows, 8)))
        accum_out_ref[j : j + 1, :] = wide[0:1, :]
        table = table_ref[j]
        updated = table * factor - learn_rate * grads * lax.rsqrt(accum)
        table_out_ref[j] = jnp.where(touched, updated, table)


def finish_body(core_ref, stay_ref, come_ref, out_ref):
    first = core_ref[0] == 0
    stay, come = stay_ref[...], come_ref[...]
    out_ref[:, 0, :] = jnp.where(first, stay, come)
    out_ref[:, 1, :] = jnp.where(first, come, stay)


def ring(value, axis, size, shift):
    return lax.ppermute(value, axis, [(i, (i + shift) % size) for i in range(size)])


def flip(value, axis, size, bit):
    return lax.ppermute(value, axis, [(i, i ^ bit) for i in range(size)])


def weight_order(x, z, core, n_x, n_z, steps_z, part):
    block = part // n_z
    third = block // 4
    line = np.arange(4 * part)
    step_x = np.array([0, -1, 1, 2])[line // part]
    step_z = np.asarray(steps_z)[(line % part) // block]
    inner = line % block
    other = inner // (2 * third)
    is_down = (inner // third) % 2
    r = inner % third
    chip = ((x + step_x + n_x) % n_x) * n_z + (z + step_z + n_z) % n_z
    owner = jnp.where(core == 0, other, 1 - other)
    target = (chip * 2 + owner) * third + r
    return jnp.stack([jnp.where(is_down == 0, target, -1), jnp.where(is_down == 1, target, -1)]).astype(i32)


def place_order(x, z, n_x, n_z, third):
    block = 4 * third
    line = np.arange(n_x * n_z * block)
    step_x, pos, inner = line // (n_z * block), line // block % n_z, line % block
    chip = (x + step_x) % n_x * n_z + (z ^ (pos // 2 + pos % 2 * (n_z // 2)))
    row = chip * 2 * third + inner % (2 * third)
    second = inner // (2 * third)
    return jnp.stack([jnp.where(second == 0, row, -1), jnp.where(second == 1, row, -1)], axis=1).astype(i32)


def on_device(
    row_table, row_accum, last_step, step_now, row_ids, row_counts, sample_slots, labels, up_weight, down_weight, out_weight
):
    n_tok, n_x, n_z = lax.axis_size("tok"), lax.axis_size("x"), lax.axis_size("z")
    _, _, width = row_table.shape
    toks, batch = sample_slots.shape
    groups, capacity = row_ids.shape[2:]
    head = width // toks
    hidden = up_weight.shape[2]
    lists = 2 * groups * capacity
    samples = 2 * batch
    core = lax.axis_index("core")
    token = lax.axis_index("tok") * 2 + core

    ids = row_ids[:, 0].transpose(0, 2, 1).reshape(2 * capacity, groups)
    looked = call(
        lookup_body,
        sds((groups, 2 * capacity, width)),
        "lookup",
        scratch=(
            pltpu.VMEM(row_table.shape, f32), pltpu.VMEM(last_step.shape, i32), pltpu.VMEM(ids.shape, i32),
            pltpu.SemaphoreType.DMA((3,)),
        ),
        n_in=4, smem=1, flops=10**9, nbytes=2 * 10**6, away=3, room=48,
    )(step_now, row_table, last_step, ids)
    sent = looked.astype(f16)
    got = lax.all_to_all(sent, ("x", "z", "core"), 0, 0, tiled=True)
    own = got.reshape(lists, width).T
    heads = lax.all_to_all(own.reshape(toks, head, lists), ("tok", "core"), 0, 0, tiled=True)
    heads = heads.reshape(width, lists).astype(f32)
    own = own.astype(f32)

    both = jnp.concatenate([up_weight, down_weight], axis=0)
    keep = jnp.where(core == 0, both[:, 0], both[:, 1])
    give = jnp.where(core == 0, both[:, 1], both[:, 0])
    piece = jnp.concatenate([keep, flip(give, "core", 2, 1)], axis=0)

    mine = jnp.concatenate([sample_slots, labels[None], jnp.zeros((toks - 1, batch), i32)], axis=0)
    theirs = flip(mine, "core", 2, 1)
    before, after = ring(piece, "z", n_z, 1), ring(piece, "z", n_z, -1)
    pair = jnp.concatenate([before, piece], axis=0)
    three = jnp.concatenate([before, piece, after], axis=0)
    far_before, far_after = ring(three, "z", n_z, 3), ring(pair, "z", n_z, -3)
    line = jnp.concatenate([three, far_before, far_after], axis=0)
    steps_z = (-1, 0, 1, -4, -3, -2, 2, 3)
    part = line.shape[0]
    x_before, x_after = ring(line, "x", n_x, 1), ring(line, "x", n_x, -1)
    far_a = ring(x_before[: part // 2], "x", n_x, 1)
    far_b = ring(x_after[part // 2 :], "x", n_x, -1)
    order = weight_order(lax.axis_index("x"), lax.axis_index("z"), core, n_x, n_z, steps_z, part)
    third = width // (n_x * n_z * 2)
    lines = n_z * 4 * third
    target = place_order(lax.axis_index("x"), lax.axis_index("z"), n_x, n_z, third)
    place = call(place_body, sds((2, n_x * lines, width), bf16), "place", n_in=1, flops=10**6, nbytes=10**6)(target)

    where = token.reshape(1).astype(i32)
    head_weight = jnp.where(core == 0, out_weight[0], out_weight[1])[:, None]
    full = (samples, hidden)
    weight = sds((width, hidden), bf16)
    normed_in, inv_in, active, slope, normed_out, inv_out, partial, up, down, targets, label_row = call(
        forward_body,
        (
            sds((width, samples)), sds((1, samples)), sds(full, bf16), sds(full),
            sds((width, samples)), sds((1, samples)), sds((1, samples)), weight, weight, sds((toks, samples), i32),
            sds((1, samples)),
        ),
        "forward",
        scratch=(
            pltpu.VMEM((4 * part, hidden), bf16), pltpu.VMEM((width, samples), f32), pltpu.VMEM((samples, width), bf16),
        ),
        n_in=12, smem=1, flops=4 * 10**9, nbytes=10**7, room=40,
    )(where, own, heads, mine, theirs, head_weight, order, line, x_before, x_after, far_a, far_b)
    logits = partial + flip(partial, "core", 2, 1)
    there = [flip(logits, "tok", n_tok, k) for k in (1, 2, 3)]
    logits = (logits + there[0]) + (there[1] + there[2])

    block = (lines, hidden // 2)
    grad_sum, grad_out, kept, *away = call(
        grad_down_body,
        (sds((width, samples)), sds((samples, width), bf16), sds(block), sds(block, bf16), sds(block, bf16), sds(block, bf16)),
        "grad_down",
        scratch=(pltpu.VMEM((2, n_x * lines, samples), bf16),),
        n_in=7, flops=2 * 10**9, nbytes=5 * 10**6,
    )(place, logits, label_row, head_weight, normed_out, inv_out, active)
    come = [ring(v, "x", n_x, k + 1) for k, v in enumerate(away)]
    pair = 8 * third
    total = kept + sum(v.astype(f32) for v in come)
    total = [total[k * pair : (k + 1) * pair] for k in range(n_z // 2)]
    total[1:] = [flip(v, "z", n_z, k + 1) for k, v in enumerate(total[1:])]
    total = (total[0] + total[1]) + (total[2] + total[3])
    stay, leave = total[: pair // 2], total[pair // 2 :]
    summed = stay + flip(leave, "z", n_z, n_z // 2)

    own_grads, head_grads = call(
        grad_rows_body,
        (sds((lists, width)), sds((width, lists), bf16)),
        "grad_rows",
        scratch=(pltpu.VMEM((width, samples), f32),),
        n_in=9, smem=1, flops=2 * 10**9, nbytes=8 * 10**6,
    )(where, targets, grad_sum, grad_out, slope, up, down, normed_in, inv_in)
    returned = lax.all_to_all(head_grads.reshape(toks, head, lists), ("tok", "core"), 0, 0, tiled=True)
    list_grads = call(
        list_body, sds((groups, 2 * capacity, width), bf16), "lists", n_in=2, flops=10**6, nbytes=10**6
    )(own_grads, returned.reshape(width, lists))
    back = lax.all_to_all(list_grads, ("x", "z", "core"), 0, 0, tiled=True)
    new_table, new_accum = call(
        update_body,
        (sds(row_table.shape), sds(row_accum.shape)),
        "update",
        n_in=7, smem=1, flops=10**9, nbytes=3 * 10**6,
    )(step_now, row_table, row_accum, last_step, ids, row_counts[:, 0], back)

    summed = jnp.concatenate([summed[: 2 * third], summed[2 * third :]], axis=1)
    low, high = summed[:third], summed[third:]
    stay, leave = jnp.where(core == 0, low, high), jnp.where(core == 0, high, low)
    come = flip(leave, "core", 2, 1)
    grad_down = call(finish_body, sds(up_weight.shape), "finish", n_in=3, smem=1, flops=10**5, nbytes=10**5)(
        core.reshape(1).astype(i32), stay, come
    )
    logits = jnp.where(core == 0, logits[0, :batch], logits[0, batch:])
    return (new_table, new_accum, grad_down, logits)


def solution(mesh):
    devices = mesh.devices.reshape(4, 4, 8, 2)
    wide = Mesh(devices, ("tok", "x", "z", "core"))
    smp = ("x", "z", "core")
    return jax.shard_map(
        on_device,
        mesh=wide,
        in_specs=(
            P("tok", smp, None),
            P("tok", smp),
            P("tok", smp),
            P(),
            P("tok", smp, None, None),
            P("tok", smp, None),
            P(None, smp),
            P(smp),
            P(smp, "tok", None),
            P(smp, "tok", None),
            P("tok", None),
        ),
        out_specs=(P("tok", smp, None), P("tok", smp), P(smp, "tok", None), P(smp)),
        check_vma=False,
    )
```

```python
import math

import jax
import jax.numpy as jnp
import numpy as np
from jax import lax
from jax.experimental import pallas as pl
from jax.experimental.pallas import tpu as pltpu
from jax.sharding import Mesh
from jax.sharding import PartitionSpec as P


decay_log = math.log(0.98)
learn_rate = 0.2
norm_eps = 1e-05
f32 = jnp.float32
bf16 = jnp.bfloat16
f16 = jnp.float16
i32 = jnp.int32


NN = (((1,), (0,)), ((), ()))
NT = (((1,), (1,)), ((), ()))
VM = pl.BlockSpec(memory_space=pltpu.VMEM)
SM = pl.BlockSpec(memory_space=pltpu.SMEM)
ANY = pl.BlockSpec(memory_space=pl.ANY)
HBM = pl.BlockSpec(memory_space=pltpu.HBM)


def dot(a, b, dims=NN):
    return lax.dot_general(a, b, dims, preferred_element_type=f32)


def split(v):
    hi = v.astype(bf16)
    return hi, (v - hi.astype(f32)).astype(bf16)


def dot2(v, b, dims=NN):
    hi, lo = split(v)
    return dot(hi, b, dims) + dot(lo, b, dims)


def iota(shape, dim):
    return lax.broadcasted_iota(i32, shape, dim)


def call(body, outs, name, scratch=(), n_in=0, smem=0, flops=0, nbytes=0, room=8, away=0):
    return pl.pallas_call(
        body,
        out_shape=outs,
        in_specs=[SM] * smem + [HBM if name == "lookup" else ANY] * away + [VM] * (n_in - smem - away),
        out_specs=jax.tree.map(lambda _: VM, outs),
        scratch_shapes=list(scratch),
        compiler_params=pltpu.CompilerParams(vmem_limit_bytes=room * 2**20),
        cost_estimate=pl.CostEstimate(flops=flops, bytes_accessed=nbytes, transcendentals=0),
    )


def sds(shape, dtype=f32):
    return jax.ShapeDtypeStruct(shape, dtype)


def slot_columns(tab, cols):
    groups = tab.shape[1]
    col = iota((1, cols), 1)
    chip, tok, grp, slot = col // 8, (col // 4) % 2, (col // 2) % 2, col % 2
    pick = (iota((groups, cols), 0) == chip * 2 + grp).astype(f32)
    every = lax.dot_general(tab, pick, NN, preferred_element_type=f32, precision=lax.Precision.HIGHEST)
    keep = iota((4, cols), 0) == tok * 2 + slot
    return jnp.sum(jnp.where(keep, every, 0.0), axis=0, keepdims=True), tok, slot


def lookup_body(step_ref, table_hbm, last_hbm, ids_hbm, out_ref, table_ref, last_ref, ids_ref, sems):
    copies = [
        pltpu.make_async_copy(source, target, sems.at[k])
        for k, (source, target) in enumerate(((ids_hbm, ids_ref), (last_hbm, last_ref), (table_hbm, table_ref)))
    ]
    for copy in copies:
        copy.start()
    toks, rows, width = table_ref.shape
    cols = out_ref.shape[0] * out_ref.shape[1]
    copies[0].wait()
    ids, tok, _ = slot_columns(ids_ref[...].astype(f32), cols)
    ids = ids + tok.astype(f32) * rows
    column = jnp.transpose(jnp.broadcast_to(ids, (8, cols)))[:, 0:1]
    copies[1].wait()
    weights = []
    for j in range(toks):
        elapsed = (step_ref[0] - last_ref[j : j + 1, :]).astype(f32)
        factor = jnp.exp(elapsed * decay_log)
        hit = iota((cols, rows), 1).astype(f32) + (j * rows) == column
        weights.append(jnp.where(hit, factor, 0.0))
    copies[2].wait()
    total = jnp.zeros((cols, width), f32)
    for j in range(toks):
        total = total + lax.dot_general(
            weights[j], table_ref[j], NN, preferred_element_type=f32, precision=lax.Precision.HIGHEST
        )
    out_ref[...] = total.reshape(out_ref.shape)


def list_targets(slots, half):
    group = (iota(slots.shape, 1) >= half).astype(i32)
    return (slots // 2) * 4 + group * 2 + slots % 2


def place_body(target_ref, place_ref):
    _, lines, width = place_ref.shape
    for k in range(2):
        place_ref[k] = (iota((lines, width), 1) == target_ref[:, k : k + 1]).astype(bf16)


def own_target(targets, token):
    return jnp.sum(jnp.where(iota(targets.shape, 0) == token, targets, 0), axis=0, keepdims=True)


def forward_body(
    where_ref, own_ref, heads_ref, mine_ref, theirs_ref, head_ref, order_ref, z_ref, xp_ref, xm_ref, xa_ref, xb_ref,
    normed_in_ref, inv_in_ref, active_ref, slope_ref, normed_out_ref, inv_out_ref, logit_ref, up_ref, down_ref,
    target_ref, label_ref, all_ref, total_ref, input_ref,
):
    start = 0
    for ref in (z_ref, xp_ref, xm_ref, xa_ref, xb_ref):
        all_ref[start : start + ref.shape[0]] = ref[...]
        start += ref.shape[0]
    width, lists = own_ref.shape
    mine, theirs = mine_ref[...], theirs_ref[...]
    first = where_ref[0] % 2 == 0
    slots = jnp.concatenate([jnp.where(first, mine, theirs), jnp.where(first, theirs, mine)], axis=1)
    samples = slots.shape[1]
    toks = slots.shape[0] // 2
    head = width // toks
    rows, hidden = all_ref.shape
    targets = list_targets(slots[0:toks, :], samples // 2)
    target_ref[...] = targets
    label_ref[...] = slots[toks : toks + 1, :].astype(f32)
    row = iota((lists, samples), 0)
    one_own = (row == own_target(targets, where_ref[0])).astype(bf16)
    own = dot2(own_ref[...], one_own)
    mixed = []
    for t in range(toks):
        one = (row == targets[t : t + 1, :]).astype(bf16)
        mixed.append(dot2(heads_ref[t * head : (t + 1) * head, :], one))
    value = own + jnp.concatenate(mixed, axis=0)
    centre = jnp.mean(value, axis=0, keepdims=True)
    shifted = value - centre
    inverse = lax.rsqrt(jnp.mean(shifted * shifted, axis=0, keepdims=True) + norm_eps)
    normed = shifted * inverse
    normed_in_ref[...] = normed
    inv_in_ref[...] = inverse
    input_ref[...] = jnp.transpose(normed.astype(bf16))
    total_ref[...] = jnp.zeros_like(total_ref)
    order_up = (iota((width, rows), 0) == order_ref[0:1, :]).astype(bf16)
    order_down = (iota((width, rows), 0) == order_ref[1:2, :]).astype(bf16)
    chunk = 256

    @pl.loop(0, hidden // chunk)
    def _(i):
        cols = pl.ds(pl.multiple_of(i * chunk, chunk), chunk)
        block = all_ref[:, cols]
        up = dot(order_up, block).astype(bf16)
        down = dot(order_down, block).astype(bf16)
        up_ref[:, cols] = up
        down_ref[:, cols] = down
        pre = dot(input_ref[...], up)
        cumulative = 0.5 * (1.0 + lax.erf(pre * (1.0 / math.sqrt(2.0))))
        density = jnp.exp(-0.5 * pre * pre) * (1.0 / math.sqrt(2.0 * math.pi))
        active = (pre * cumulative).astype(bf16)
        active_ref[:, cols] = active
        slope_ref[:, cols] = cumulative + pre * density
        total_ref[...] += dot(down, active, NT)

    value = normed_in_ref[...] + total_ref[...]
    centre = jnp.mean(value, axis=0, keepdims=True)
    shifted = value - centre
    inverse = lax.rsqrt(jnp.mean(shifted * shifted, axis=0, keepdims=True) + norm_eps)
    normed = shifted * inverse
    normed_out_ref[...] = normed
    inv_out_ref[...] = inverse
    logit_ref[...] = jnp.sum(normed * head_ref[...], axis=0, keepdims=True)


def norm_back(grad_in, normed, inverse):
    first = jnp.mean(grad_in, axis=0, keepdims=True)
    second = jnp.mean(grad_in * normed, axis=0, keepdims=True)
    return inverse * (grad_in - first - normed * second)


def grad_down_body(
    place_ref, logit_ref, label_ref, head_ref, normed_out_ref, inv_out_ref, active_ref,
    grad_sum_ref, grad_out_ref, kept_ref, next_ref, far_ref, last_ref, padded_ref,
):
    dlogit = jax.nn.sigmoid(logit_ref[...]) - label_ref[...]
    grad = norm_back(dlogit * head_ref[...], normed_out_ref[...], inv_out_ref[...])
    grad_sum_ref[...] = grad
    rounded = grad.astype(bf16)
    grad_out_ref[...] = jnp.transpose(rounded)
    lines, half = kept_ref.shape
    for k in range(2):
        padded_ref[k] = dot(place_ref[k], rounded).astype(bf16)
    chunk = 256

    @pl.loop(0, half // chunk)
    def _(i):
        cols = pl.ds(pl.multiple_of(i * chunk, chunk), chunk)
        more = pl.ds(pl.multiple_of(half + i * chunk, chunk), chunk)
        value = dot(padded_ref[0], active_ref[:, cols]) + dot(padded_ref[1], active_ref[:, more])
        kept_ref[:, cols] = value[0:lines]
        next_ref[:, cols] = value[lines : 2 * lines].astype(bf16)
        far_ref[:, cols] = value[2 * lines : 3 * lines].astype(bf16)
        last_ref[:, cols] = value[3 * lines :].astype(bf16)


def grad_rows_body(
    where_ref, target_ref, grad_sum_ref, grad_out_ref, slope_ref, up_ref, down_ref, normed_in_ref, inv_in_ref,
    own_ref, back_ref, total_ref,
):
    lists, width = own_ref.shape
    toks, samples = target_ref.shape
    head = width // toks
    total_ref[...] = grad_sum_ref[...]
    chunk = 256

    @pl.loop(0, slope_ref.shape[1] // chunk)
    def _(i):
        cols = pl.ds(pl.multiple_of(i * chunk, chunk), chunk)
        grad = dot(grad_out_ref[...], down_ref[:, cols])
        grad_pre = (grad * slope_ref[:, cols]).astype(bf16)
        total_ref[...] += dot(up_ref[:, cols], grad_pre, NT)

    mixed = norm_back(total_ref[...], normed_in_ref[...], inv_in_ref[...])
    targets = target_ref[...]
    row = iota((lists, samples), 0)
    one_own = (row == own_target(targets, where_ref[0])).astype(bf16)
    hi, lo = split(mixed)
    own_ref[...] = dot(one_own, hi, NT) + dot(one_own, lo, NT)
    for t in range(toks):
        one = (row == targets[t : t + 1, :]).astype(bf16)
        span = slice(t * head, (t + 1) * head)
        back_ref[span, :] = (dot(hi[span], one, NT) + dot(lo[span], one, NT)).astype(bf16)


def list_body(own_ref, returned_ref, out_ref):
    returned = jnp.transpose(returned_ref[...].astype(f32))
    out_ref[...] = (own_ref[...] + returned).astype(bf16).reshape(out_ref.shape)


def update_body(
    step_ref, table_ref, accum_ref, last_ref, ids_ref, counts_ref, back_ref,
    table_out_ref, accum_out_ref,
):
    toks, rows, width = table_ref.shape
    cols = back_ref.shape[0] * back_ref.shape[1]
    ids, tok, slot = slot_columns(ids_ref[...].astype(f32), cols)
    counts = counts_ref[...].astype(f32)
    four = jnp.concatenate([counts[0:1], counts[0:1], counts[1:2], counts[1:2]], axis=0)
    have, _, _ = slot_columns(four, cols)
    valid = slot.astype(f32) < have
    row = iota((rows, cols), 0).astype(f32)
    back = back_ref[...].astype(f32).reshape(cols, width).astype(bf16)
    for j in range(toks):
        named = jnp.where((tok == j) & valid, ids, -1.0)
        hit = (row == named).astype(f32)
        grads = dot(hit.astype(bf16), back)
        square = grads * grads
        touched = jnp.max(hit, axis=1, keepdims=True) > 0.0
        flat = jnp.concatenate(
            [last_ref[j : j + 1, :].astype(f32), accum_ref[j : j + 1, :], jnp.zeros((6, rows), f32)], axis=0
        )
        upright = jnp.transpose(flat)
        factor = jnp.exp((step_ref[0].astype(f32) - upright[:, 0:1]) * decay_log)
        accum = upright[:, 1:2] + jnp.mean(square, axis=1, keepdims=True)
        wide = jnp.transpose(jnp.broadcast_to(accum, (rows, 8)))
        accum_out_ref[j : j + 1, :] = wide[0:1, :]
        table = table_ref[j]
        updated = table * factor - learn_rate * grads * lax.rsqrt(accum)
        table_out_ref[j] = jnp.where(touched, updated, table)


def finish_body(core_ref, stay_ref, come_ref, out_ref):
    first = core_ref[0] == 0
    stay, come = stay_ref[...], come_ref[...]
    out_ref[:, 0, :] = jnp.where(first, stay, come)
    out_ref[:, 1, :] = jnp.where(first, come, stay)


def ring(value, axis, size, shift):
    return lax.ppermute(value, axis, [(i, (i + shift) % size) for i in range(size)])


def flip(value, axis, size, bit):
    return lax.ppermute(value, axis, [(i, i ^ bit) for i in range(size)])


def weight_order(x, z, core, n_x, n_z, steps_z, part):
    block = part // n_z
    third = block // 4
    line = np.arange(4 * part)
    step_x = np.array([0, -1, 1, 2])[line // part]
    step_z = np.asarray(steps_z)[(line % part) // block]
    inner = line % block
    other = inner // (2 * third)
    is_down = (inner // third) % 2
    r = inner % third
    chip = ((x + step_x + n_x) % n_x) * n_z + (z + step_z + n_z) % n_z
    owner = jnp.where(core == 0, other, 1 - other)
    target = (chip * 2 + owner) * third + r
    return jnp.stack([jnp.where(is_down == 0, target, -1), jnp.where(is_down == 1, target, -1)]).astype(i32)


def place_order(x, z, n_x, n_z, third):
    block = 4 * third
    line = np.arange(n_x * n_z * block)
    step_x, pos, inner = line // (n_z * block), line // block % n_z, line % block
    chip = (x + step_x) % n_x * n_z + (z ^ (pos // 2 + pos % 2 * (n_z // 2)))
    row = chip * 2 * third + inner % (2 * third)
    second = inner // (2 * third)
    return jnp.stack([jnp.where(second == 0, row, -1), jnp.where(second == 1, row, -1)], axis=1).astype(i32)


def on_device(
    row_table, row_accum, last_step, step_now, row_ids, row_counts, sample_slots, labels, up_weight, down_weight, out_weight
):
    n_tok, n_x, n_z = lax.axis_size("tok"), lax.axis_size("x"), lax.axis_size("z")
    _, _, width = row_table.shape
    toks, batch = sample_slots.shape
    groups, capacity = row_ids.shape[2:]
    head = width // toks
    hidden = up_weight.shape[2]
    lists = 2 * groups * capacity
    samples = 2 * batch
    core = lax.axis_index("core")
    token = lax.axis_index("tok") * 2 + core

    ids = row_ids[:, 0].transpose(0, 2, 1).reshape(2 * capacity, groups)
    looked = call(
        lookup_body,
        sds((groups, 2 * capacity, width)),
        "lookup",
        scratch=(
            pltpu.VMEM(row_table.shape, f32), pltpu.VMEM(last_step.shape, i32), pltpu.VMEM(ids.shape, i32),
            pltpu.SemaphoreType.DMA((3,)),
        ),
        n_in=4, smem=1, flops=10**9, nbytes=2 * 10**6, away=3, room=48,
    )(step_now, row_table, last_step, ids)
    sent = looked.astype(f16)
    got = lax.all_to_all(sent, ("x", "z", "core"), 0, 0, tiled=True)
    own = got.reshape(lists, width).T
    heads = lax.all_to_all(own.reshape(toks, head, lists), ("tok", "core"), 0, 0, tiled=True)
    heads = heads.reshape(width, lists).astype(f32)
    own = own.astype(f32)

    both = jnp.concatenate([up_weight, down_weight], axis=0)
    keep = jnp.where(core == 0, both[:, 0], both[:, 1])
    give = jnp.where(core == 0, both[:, 1], both[:, 0])
    piece = jnp.concatenate([keep, flip(give, "core", 2, 1)], axis=0)

    mine = jnp.concatenate([sample_slots, labels[None], jnp.zeros((toks - 1, batch), i32)], axis=0)
    theirs = flip(mine, "core", 2, 1)
    before, after = ring(piece, "z", n_z, 1), ring(piece, "z", n_z, -1)
    pair = jnp.concatenate([before, piece], axis=0)
    three = jnp.concatenate([before, piece, after], axis=0)
    far_before, far_after = ring(three, "z", n_z, 3), ring(pair, "z", n_z, -3)
    line = jnp.concatenate([three, far_before, far_after], axis=0)
    steps_z = (-1, 0, 1, -4, -3, -2, 2, 3)
    part = line.shape[0]
    x_before, x_after = ring(line, "x", n_x, 1), ring(line, "x", n_x, -1)
    far_a = ring(x_before[: part // 2], "x", n_x, 1)
    far_b = ring(x_after[part // 2 :], "x", n_x, -1)
    order = weight_order(lax.axis_index("x"), lax.axis_index("z"), core, n_x, n_z, steps_z, part)
    third = width // (n_x * n_z * 2)
    lines = n_z * 4 * third
    target = place_order(lax.axis_index("x"), lax.axis_index("z"), n_x, n_z, third)
    place = call(place_body, sds((2, n_x * lines, width), bf16), "place", n_in=1, flops=10**6, nbytes=10**6)(target)

    where = token.reshape(1).astype(i32)
    head_weight = jnp.where(core == 0, out_weight[0], out_weight[1])[:, None]
    full = (samples, hidden)
    weight = sds((width, hidden), bf16)
    normed_in, inv_in, active, slope, normed_out, inv_out, partial, up, down, targets, label_row = call(
        forward_body,
        (
            sds((width, samples)), sds((1, samples)), sds(full, bf16), sds(full),
            sds((width, samples)), sds((1, samples)), sds((1, samples)), weight, weight, sds((toks, samples), i32),
            sds((1, samples)),
        ),
        "forward",
        scratch=(
            pltpu.VMEM((4 * part, hidden), bf16), pltpu.VMEM((width, samples), f32), pltpu.VMEM((samples, width), bf16),
        ),
        n_in=12, smem=1, flops=4 * 10**9, nbytes=10**7, room=40,
    )(where, own, heads, mine, theirs, head_weight, order, line, x_before, x_after, far_a, far_b)
    logits = partial + flip(partial, "core", 2, 1)
    there = [flip(logits, "tok", n_tok, k) for k in (1, 2, 3)]
    logits = (logits + there[0]) + (there[1] + there[2])

    block = (lines, hidden // 2)
    grad_sum, grad_out, kept, *away = call(
        grad_down_body,
        (sds((width, samples)), sds((samples, width), bf16), sds(block), sds(block, bf16), sds(block, bf16), sds(block, bf16)),
        "grad_down",
        scratch=(pltpu.VMEM((2, n_x * lines, samples), bf16),),
        n_in=7, flops=2 * 10**9, nbytes=5 * 10**6,
    )(place, logits, label_row, head_weight, normed_out, inv_out, active)
    come = [ring(v, "x", n_x, k + 1) for k, v in enumerate(away)]
    pair = 8 * third
    total = kept + sum(v.astype(f32) for v in come)
    total = [total[k * pair : (k + 1) * pair] for k in range(n_z // 2)]
    total[1:] = [flip(v, "z", n_z, k + 1) for k, v in enumerate(total[1:])]
    total = (total[0] + total[1]) + (total[2] + total[3])
    stay, leave = total[: pair // 2], total[pair // 2 :]
    summed = stay + flip(leave, "z", n_z, n_z // 2)

    own_grads, head_grads = call(
        grad_rows_body,
        (sds((lists, width)), sds((width, lists), bf16)),
        "grad_rows",
        scratch=(pltpu.VMEM((width, samples), f32),),
        n_in=9, smem=1, flops=2 * 10**9, nbytes=8 * 10**6,
    )(where, targets, grad_sum, grad_out, slope, up, down, normed_in, inv_in)
    returned = lax.all_to_all(head_grads.reshape(toks, head, lists), ("tok", "core"), 0, 0, tiled=True)
    list_grads = call(
        list_body, sds((groups, 2 * capacity, width), bf16), "lists", n_in=2, flops=10**6, nbytes=10**6
    )(own_grads, returned.reshape(width, lists))
    back = lax.all_to_all(list_grads, ("x", "z", "core"), 0, 0, tiled=True)
    new_table, new_accum = call(
        update_body,
        (sds(row_table.shape), sds(row_accum.shape)),
        "update",
        n_in=7, smem=1, flops=10**9, nbytes=3 * 10**6,
    )(step_now, row_table, row_accum, last_step, ids, row_counts[:, 0], back)

    summed = jnp.concatenate([summed[: 2 * third], summed[2 * third :]], axis=1)
    low, high = summed[:third], summed[third:]
    stay, leave = jnp.where(core == 0, low, high), jnp.where(core == 0, high, low)
    come = flip(leave, "core", 2, 1)
    grad_down = call(finish_body, sds(up_weight.shape), "finish", n_in=3, smem=1, flops=10**5, nbytes=10**5)(
        core.reshape(1).astype(i32), stay, come
    )
    logits = jnp.where(core == 0, logits[0, :batch], logits[0, batch:])
    return (new_table, new_accum, grad_down, logits)


def solution(mesh):
    devices = mesh.devices.reshape(4, 4, 8, 2)
    wide = Mesh(devices, ("tok", "x", "z", "core"))
    smp = ("x", "z", "core")
    return jax.shard_map(
        on_device,
        mesh=wide,
        in_specs=(
            P("tok", smp, None),
            P("tok", smp),
            P("tok", smp),
            P(),
            P("tok", smp, None, None),
            P("tok", smp, None),
            P(None, smp),
            P(smp),
            P(smp, "tok", None),
            P(smp, "tok", None),
            P("tok", None),
        ),
        out_specs=(P("tok", smp, None), P("tok", smp), P(smp, "tok", None), P(smp)),
        check_vma=False,
    )
```
